32 devices in a mesh: groups: 2 (over y), seq: 1, mp: 8 (over z, x), section: 2 (over core).
Axes of the slice: x: 2, y: 2, z: 4, core: 2. Of those that a mesh axis runs over, the one named last changes fastest.
Arguments:
- latent: bfloat16 [1024, 3072], P(('groups', 'seq', 'section'), 'mp'), parts along dimension 0, may hold values from -6 to 6
- t_index: int32 [2], P('groups'), parts along dimension 0, may hold values from 0 to 27
- mod_table: bfloat16 [28, 3, 3072], P(None, None, 'mp'), may hold values from -1 to 4
- w_qkv: bfloat16 [3072, 6144], P('section', 'mp'), may hold values from -1 to 1
- w_out: bfloat16 [2048, 3072], P('section', 'mp'), may hold values from -0.125 to 0.125
Outputs:
- updated: bfloat16 [1024, 3072], P(('groups', 'seq', 'section'), 'mp'), parts along dimension 0
The draws below stay inside these ranges and needn't reach their ends.
There are 2 independent parts, one for each index of `groups`. The reference program is written for one: setup_inputs(seed, part) draws one part's arguments, and reference() takes and returns one part's arrays. A program takes and returns all parts, laid end to end along the dimension named above; an argument that names none is the same for every part. Nothing has to cross between parts.
Inputs may be any that keep to these rules, and one draw needn't show every extreme that they name: `t_index`: the index of the current step among 28.
All inputs are finite; a program needn't handle non-finite values.
Results may differ from the reference program's by a relative error of at most 0.0085.
The reference program's roundings to bfloat16 on the way (of `modulated`, `projected` and `attended`) count: a program that leaves them out, or rounds other values in their place, can miss the bound.
Values may be sent and summed in bfloat16 or wider, within the bound.
A program may use at most 128 MiB of HBM per device.

```python
import math
import jax
import jax.numpy as jnp
from jax import lax

D = 3072
HEADS = 16
HEAD_DIM = 128
STEPS = 28
SEQ_LEN = 512


def draw_latent(key, part):
    key_own = jax.random.fold_in(key, 11)
    own = jax.random.normal(key_own, (SEQ_LEN, D), jnp.float32)
    return jnp.clip(own, -6.0, 6.0).astype(jnp.bfloat16)


def draw_mod_table(key, part):
    key_shift, key_scale, key_gate = jax.random.split(key, 3)
    shift_rows = jax.random.uniform(key_shift, (STEPS, 1, D), jnp.float32, -1.0, 1.0)
    scale_rows = jax.random.uniform(key_scale, (STEPS, 1, D), jnp.float32, -0.5, 4.0)
    gate_rows = jax.random.uniform(key_gate, (STEPS, 1, D), jnp.float32, 0.5, 2.0)
    return jnp.concatenate([shift_rows, scale_rows, gate_rows], axis=1).astype(jnp.bfloat16)


def draw_w_qkv(key, part):
    key_values = jax.random.fold_in(jax.random.fold_in(key, 23), 0)
    raw_values = jnp.clip(jax.random.normal(key_values, (D, HEADS, 3, HEAD_DIM), jnp.float32), -6.0, 6.0)
    aligned = raw_values[:, :, 1]
    raw_values = jnp.stack([raw_values[:, :, 0], aligned, raw_values[:, :, 2]], axis=2)
    return (raw_values.reshape(D, HEADS * 3 * HEAD_DIM) / math.sqrt(D)).astype(jnp.bfloat16)


def shard_levels(rng, extent, pieces, least, largest):
    def one(position, parts):
        draws = jax.random.uniform(jax.random.fold_in(jax.random.fold_in(rng, 6), position), (parts,), jnp.float32, least / len(pieces), largest / len(pieces))
        return jnp.repeat(jnp.exp(draws), extent[position] // parts).reshape((-1,) + (1,) * (len(extent) - position - 1))

    factor_of = one(*pieces[0])
    for cut in pieces[1:]:
        factor_of = factor_of * one(*cut)
    return factor_of


def bell_draw(own_key, dims, spread, reach, cuts=(), kind=jnp.bfloat16):
    loudness = shard_levels(own_key, dims, cuts, -0.22, 0.18) if cuts else 1.0
    result = jax.random.normal(own_key, dims, jnp.float32) * spread * loudness
    return jnp.minimum(jnp.maximum(result, -reach), reach).astype(kind)


def setup_inputs(seed: int = 0, part: int = 0) -> dict:
    streams_of = jax.random.split(jax.random.key(seed), 6)
    own_keys = jax.random.split(jax.random.fold_in(streams_of[5], part), 6)
    latent = draw_latent(jax.random.fold_in(jax.random.fold_in(streams_of[5], part), 71), part)
    t_index = jax.random.randint(own_keys[1], (1,), 0, STEPS).astype(jnp.int32)
    mod_table = draw_mod_table(jax.random.fold_in(streams_of[5], 71), part)
    w_qkv = draw_w_qkv(jax.random.fold_in(streams_of[5], 71), part)
    w_out = bell_draw(streams_of[4], (HEADS * HEAD_DIM, D), (HEADS * HEAD_DIM) ** -0.5, 0.125, ((0, 2), (1, 8)))
    return {"latent": latent, "t_index": t_index, "mod_table": mod_table, "w_qkv": w_qkv, "w_out": w_out}


def layer_normed(values):
    mean_row = lax.optimization_barrier(jnp.mean(values, axis=-1, keepdims=True))
    centred = values - mean_row
    variance = lax.optimization_barrier(jnp.mean(centred * centred, axis=-1, keepdims=True))
    return centred * lax.rsqrt(variance + 1e-06)

def one_head(head_parts):
    queries = head_parts[0]
    key_rows = head_parts[1]
    value_rows = head_parts[2]
    scores = jnp.dot(queries, key_rows.T, preferred_element_type=jnp.float32) * (1.0 / math.sqrt(HEAD_DIM))
    weights = jnp.exp(scores - lax.optimization_barrier(jnp.max(scores, axis=-1, keepdims=True)))
    numerator = jnp.dot(weights.astype(jnp.bfloat16), value_rows, preferred_element_type=jnp.float32)
    return (numerator / lax.optimization_barrier(jnp.sum(weights, axis=-1, keepdims=True))).astype(jnp.bfloat16)

def reference(latent, t_index, mod_table, w_qkv, w_out):
    mod_row = lax.dynamic_index_in_dim(mod_table, t_index[0], 0, keepdims=False).astype(jnp.float32)
    base = latent.astype(jnp.float32)
    modulated = (layer_normed(base) * (1.0 + mod_row[1]) + mod_row[0]).astype(jnp.bfloat16)
    projected = jnp.dot(modulated, w_qkv, preferred_element_type=jnp.float32).astype(jnp.bfloat16)
    token_count = projected.shape[0]
    grouped = projected.reshape(token_count, HEADS, 3, HEAD_DIM).transpose(1, 2, 0, 3)
    attended = lax.map(one_head, grouped)
    flat = attended.transpose(1, 0, 2).reshape(token_count, HEADS * HEAD_DIM)
    mixed_rows = jnp.dot(flat, w_out, preferred_element_type=jnp.float32)
    return (base + mod_row[2] * mixed_rows).astype(jnp.bfloat16)
```

```python
import functools
import math

import jax
import jax.numpy as jnp
from jax import lax
from jax.experimental import pallas as pl
from jax.experimental.pallas import tpu as pltpu
from jax.sharding import PartitionSpec as P

HEAD_DIM = 128
LANES = 128
WIDE = 2
CHUNKS = (2, 2)
MESH = pl.DeviceIdType.MESH


def layer_normed(values):
    mean_row = jnp.mean(values, axis=-1, keepdims=True)
    centred = values - mean_row
    variance = jnp.mean(centred * centred, axis=-1, keepdims=True)
    return centred * lax.rsqrt(variance + 1e-06)


def local(latent, t_index, mod_table, w_qkv, w_out):
    mod_local = lax.dynamic_index_in_dim(mod_table, t_index[0], 0, keepdims=False)
    features, mod_whole = (
        lax.all_gather(latent, "mp", axis=1, tiled=True),
        lax.all_gather(mod_local, "mp", axis=1, tiled=True),
    )
    mod_float = mod_whole.astype(jnp.float32)
    modulated = (
        layer_normed(features.astype(jnp.float32)) * (1.0 + mod_float[1]) + mod_float[0]
    ).astype(jnp.bfloat16)
    tok_rows = latent.shape[0]
    heads_dev = w_qkv.shape[1] // (3 * HEAD_DIM)
    qkv_full, out_full = (
        lax.all_gather(w_qkv, "section", axis=0, tiled=True),
        lax.all_gather(w_out, "section", axis=0, tiled=True),
    )
    projected = jnp.dot(modulated, qkv_full, preferred_element_type=jnp.float32).astype(
        jnp.bfloat16
    )
    grouped = projected.reshape(tok_rows, heads_dev, 3, HEAD_DIM)
    queries = grouped[:, :, 0]
    key_rows = grouped[:, :, 1]
    value_rows = grouped[:, :, 2]
    scale_factor = 1.0 / math.sqrt(HEAD_DIM)
    initial = (
        jnp.full((tok_rows, heads_dev), -1e30, jnp.float32),
        jnp.zeros((tok_rows, heads_dev), jnp.float32),
        jnp.zeros((tok_rows, heads_dev, HEAD_DIM), jnp.float32),
    )
    key_piece = lax.all_gather(key_rows, ("seq", "section"), axis=0, tiled=True)
    value_piece = lax.all_gather(value_rows, ("seq", "section"), axis=0, tiled=True)
    total_rows = key_piece.shape[0]
    block_rows = math.gcd(total_rows, 1024)

    def one_block(block_index, carried_block):
        running, totals, weighted = carried_block
        key_block = lax.dynamic_slice_in_dim(key_piece, block_index * block_rows, block_rows, 0)
        value_block = lax.dynamic_slice_in_dim(value_piece, block_index * block_rows, block_rows, 0)
        scores = (
            jnp.einsum("thd,khd->thk", queries, key_block, preferred_element_type=jnp.float32)
            * scale_factor
        )
        newest = jnp.maximum(running, jnp.max(scores, axis=-1))
        factor = jnp.exp(running - newest)
        weights = jnp.exp(scores - newest[..., None])
        totals = totals * factor + jnp.sum(weights, axis=-1)
        weighted = weighted * factor[..., None] + jnp.einsum(
            "thk,khd->thd",
            weights.astype(jnp.bfloat16),
            value_block,
            preferred_element_type=jnp.float32,
        )
        return (newest, totals, weighted)

    finished = lax.fori_loop(0, total_rows // block_rows, one_block, initial)
    attended = (
        (finished[2] / finished[1][..., None])
        .astype(jnp.bfloat16)
        .reshape(tok_rows, heads_dev * HEAD_DIM)
    )
    mixed_rows = jnp.dot(
        lax.all_gather(attended, "mp", axis=1, tiled=True),
        out_full,
        preferred_element_type=jnp.float32,
    )
    return (latent.astype(jnp.float32) + mod_local[2].astype(jnp.float32) * mixed_rows).astype(
        jnp.bfloat16
    )


def fused_kernel(
    n,
    x_hbm,
    t_ref,
    mod_hbm,
    wq_hbm,
    wo_hbm,
    out_ref,
    xs,
    table,
    small,
    wq,
    wo,
    acc,
    stat,
    proj,
    pkv,
    att,
    mixed,
    own_sem,
    table_sem,
    ssem,
    rsem,
    small_send,
    small_recv,
    wq_sem,
    wq_send,
    wo_sem,
    wo_send,
    kv_send,
    kv_recv,
):
    me = lax.axis_index("mp")
    sec = lax.axis_index("section")
    other = 1 - sec
    deep = n // WIDE
    z, x = me // WIDE, me % WIDE
    rows, feats = x_hbm.shape
    piece_q = wq.shape[1]
    per_sec = n // 2
    piece_o = wo.shape[1]
    heads = att.shape[2] // HEAD_DIM

    own_copy = pltpu.make_async_copy(x_hbm, xs.at[me], own_sem)
    own_copy.start()
    table_copy = pltpu.make_async_copy(mod_hbm, table, table_sem)
    table_copy.start()

    barrier = pltpu.get_barrier_semaphore()
    for step in range(1, n):
        pl.semaphore_signal(
            barrier, inc=1, device_id={"mp": lax.rem(me + step, n)}, device_id_type=MESH
        )
    pl.semaphore_signal(barrier, inc=1, device_id={"section": other}, device_id_type=MESH)

    def wq_local(i):
        p = sec * per_sec + i
        return pltpu.make_async_copy(
            wq_hbm.at[pl.ds(i * piece_q, piece_q)], wq.at[p], wq_sem.at[p]
        )

    def wo_local(i):
        return pltpu.make_async_copy(
            wo_hbm.at[pl.ds(i * piece_o, piece_o)],
            wo.at[sec * per_sec + i],
            wo_sem.at[sec * per_sec + i],
        )

    for i in range(per_sec):
        wq_local(i).start()
    for i in range(per_sec):
        wo_local(i).start()

    own_copy.wait()
    mine = xs[me].astype(jnp.float32)
    table_copy.wait()

    def mod_row(j):
        entries = table[j].astype(jnp.float32)
        steps = lax.broadcasted_iota(jnp.int32, entries.shape, 0)
        chosen = jnp.where(steps == t_ref[0], entries, 0.0)
        return jnp.sum(chosen, axis=0, keepdims=True)

    mean_col = jnp.sum(mine, axis=1, keepdims=True) * (1.0 / feats)
    off = mine - mean_col
    m2_col = jnp.sum(off * off, axis=1, keepdims=True)
    mean_row = jnp.broadcast_to(mean_col, (rows, LANES)).T[0:1, :]
    m2_row = jnp.broadcast_to(m2_col, (rows, LANES)).T[0:1, :]
    small[me, 0:1, :] = mod_row(0)
    small[me, 1:2, :] = 1.0 + mod_row(1)
    small[me, 2:3, 0:rows] = mean_row
    small[me, 3:4, 0:rows] = m2_row

    pl.semaphore_wait(barrier, n)

    def small_copy(step):
        return pltpu.make_async_remote_copy(
            src_ref=small.at[me],
            dst_ref=small.at[me],
            send_sem=small_send.at[step],
            recv_sem=small_recv.at[me],
            device_id={"mp": lax.rem(me + step, n)},
            device_id_type=MESH,
        )

    def chunk(phase, src, h):
        if phase == 0:
            part = rows // CHUNKS[0]
            return xs.at[src, pl.ds(h * part, part), :]
        split = CHUNKS[1] // heads
        part = rows // split
        return att.at[
            src, pl.ds(h % split * part, part), pl.ds(h // split * HEAD_DIM, HEAD_DIM)
        ]

    def route(src):
        sz, sx = src // WIDE, src % WIDE
        same = sx == x
        up = jnp.logical_and(same, jnp.logical_and(sz <= z, z + 1 < deep))
        down = jnp.logical_and(same, jnp.logical_and(sz >= z, z > 0))
        across = same
        return (
            (2, across, z * WIDE + (1 - x)),
            (0, up, me + WIDE),
            (1, down, me - WIDE),
        )

    def hop(phase, src, h, direction, target):
        return pltpu.make_async_remote_copy(
            src_ref=chunk(phase, src, h),
            dst_ref=chunk(phase, src, h),
            send_sem=ssem.at[phase, direction, src, h],
            recv_sem=rsem.at[phase, src, h],
            device_id={"mp": target},
            device_id_type=MESH,
        )

    def relay(phase, src, h):
        for direction, wanted, target in route(src):

            @pl.when(wanted)
            def _():
                hop(phase, src, h, direction, target).start()

    def arrive(phase, src, h):
        hop(phase, src, h, 0, me).wait_recv()
        relay(phase, src, h)

    relay(0, me, 0)
    for step in range(1, n):
        small_copy(step).start()
    for h in range(1, CHUNKS[0]):
        relay(0, me, h)

    def wq_remote(i):
        p = sec * per_sec + i
        return pltpu.make_async_remote_copy(
            src_ref=wq_hbm.at[pl.ds(i * piece_q, piece_q)],
            dst_ref=wq.at[p],
            send_sem=wq_send.at[i],
            recv_sem=wq_sem.at[p],
            device_id={"section": other},
            device_id_type=MESH,
        )

    def wo_remote(i):
        p = sec * per_sec + i
        return pltpu.make_async_remote_copy(
            src_ref=wo_hbm.at[pl.ds(i * piece_o, piece_o)],
            dst_ref=wo.at[p],
            send_sem=wo_send.at[i],
            recv_sem=wo_sem.at[p],
            device_id={"section": other},
            device_id_type=MESH,
        )

    for i in range(per_sec):
        wq_remote(i).start()
    for i in range(per_sec):
        wo_remote(i).start()

    def receive(phase, d):
        where = []
        for sign in (1, -1):
            sz = z + sign * d
            where.append((sz * WIDE + x, jnp.logical_and(sz >= 0, sz < deep)))
        for h in range(CHUNKS[phase]):
            for src, there in where:

                @pl.when(there)
                def _():
                    arrive(phase, src, h)

    def consume(phase, d, use):
        def one(i, carry_in):
            col = i < 2
            sign = 1 - 2 * lax.rem(i, 2)
            sz = z + sign * jnp.where(col, d, d - 1)
            there = jnp.logical_and(sz >= 0, sz < deep)
            there = jnp.logical_and(there, jnp.logical_or(i < 3, d > 1))
            src = sz * WIDE + jnp.where(col, x, 1 - x)

            @pl.when(jnp.logical_and(there, i >= 2))
            def _():
                for h in range(CHUNKS[phase]):
                    hop(phase, src, h, 0, me).wait_recv()

            @pl.when(there)
            def _():
                use(src)

            return carry_in

        lax.fori_loop(0, 4, one, 0)

    def sweep(phase, use):
        def early(d, carry):
            receive(phase, d)
            consume(phase, d - 1, use)
            return carry

        lax.fori_loop(2, deep, early, 0)
        consume(phase, deep - 1, use)
        consume(phase, deep, use)

    receive(0, 1)

    for step in range(1, n):
        p = lax.rem(me + step, n)
        pltpu.make_async_copy(small.at[p], small.at[p], small_recv.at[p]).wait()
    total = jnp.zeros((1, rows), jnp.float32)
    for p in range(n):
        total = total + small[p, 2:3, 0:rows]
    grand = total * (1.0 / n)
    m2 = jnp.zeros((1, rows), jnp.float32)
    for p in range(n):
        gap = small[p, 2:3, 0:rows] - grand
        m2 = m2 + small[p, 3:4, 0:rows] + feats * (gap * gap)
    inv = lax.rsqrt(m2 * (1.0 / (n * feats)) + 1e-06)
    stat[0] = jnp.broadcast_to(grand, (LANES, rows)).T
    stat[1] = jnp.broadcast_to(inv, (LANES, rows)).T

    def project(src):
        pltpu.make_async_copy(wq.at[src], wq.at[src], wq_sem.at[src]).wait()
        mean, rstd = stat[0], stat[1]
        shift_scale = small[src, 0:2, :]
        parts = []
        for c in range(feats // LANES):
            cols = slice(c * LANES, (c + 1) * LANES)
            values = xs[src, :, cols].astype(jnp.float32)
            parts.append(
                ((values - mean) * rstd * shift_scale[1:2, cols] + shift_scale[0:1, cols]).astype(
                    jnp.bfloat16
                )
            )
        return jnp.dot(
            jnp.concatenate(parts, axis=1), wq[src], preferred_element_type=jnp.float32
        )

    acc[...] = project(me)

    def use_projection(src):
        acc[...] += project(src)

    sweep(0, use_projection)

    def kv_copy(h):
        return pltpu.make_async_remote_copy(
            src_ref=proj.at[:, pl.ds((3 * h + 1) * HEAD_DIM, 2 * HEAD_DIM)],
            dst_ref=pkv.at[h],
            send_sem=kv_send.at[h],
            recv_sem=kv_recv.at[h],
            device_id={"section": other},
            device_id_type=MESH,
        )

    for h in range(heads):
        cols = slice((3 * h + 1) * HEAD_DIM, (3 * h + 3) * HEAD_DIM)
        proj[:, cols] = acc[:, cols].astype(jnp.bfloat16)
        kv_copy(h).start()

    factor = 1.0 / math.sqrt(HEAD_DIM)
    contract = (((1,), (1,)), ((), ()))
    for h in range(heads):
        base = 3 * h * HEAD_DIM
        queries = acc[:, base : base + HEAD_DIM].astype(jnp.bfloat16)
        own_k = proj[:, base + HEAD_DIM : base + 2 * HEAD_DIM]
        own_v = proj[:, base + 2 * HEAD_DIM : base + 3 * HEAD_DIM]
        s_own = lax.dot_general(queries, own_k, contract, preferred_element_type=jnp.float32) * factor
        kv_copy(h).wait_recv()
        far_k = pkv[h, :, 0:HEAD_DIM]
        far_v = pkv[h, :, HEAD_DIM : 2 * HEAD_DIM]
        s_far = lax.dot_general(queries, far_k, contract, preferred_element_type=jnp.float32) * factor
        top = jnp.maximum(
            jnp.max(s_own, axis=1, keepdims=True), jnp.max(s_far, axis=1, keepdims=True)
        )
        e_own = jnp.exp(s_own - top)
        e_far = jnp.exp(s_far - top)
        norm = jnp.sum(e_own, axis=1, keepdims=True) + jnp.sum(e_far, axis=1, keepdims=True)
        weighted = jnp.dot(
            e_own.astype(jnp.bfloat16), own_v, preferred_element_type=jnp.float32
        ) + jnp.dot(e_far.astype(jnp.bfloat16), far_v, preferred_element_type=jnp.float32)
        att[me, :, h * HEAD_DIM : (h + 1) * HEAD_DIM] = (weighted / norm).astype(jnp.bfloat16)
        for c in range(CHUNKS[1] // heads):
            relay(1, me, h * (CHUNKS[1] // heads) + c)

    def mix(src):
        pltpu.make_async_copy(wo.at[src], wo.at[src], wo_sem.at[src]).wait()
        return jnp.dot(att[src], wo[src], preferred_element_type=jnp.float32)

    receive(1, 1)
    mixed[...] = mix(me)

    def use_mix(src):
        mixed[...] += mix(src)

    sweep(1, use_mix)

    gate = mod_row(2)
    out_ref[...] = (xs[me].astype(jnp.float32) + gate * mixed[...]).astype(jnp.bfloat16)

    for step in range(1, n):
        small_copy(step).wait_send()
    for i in range(per_sec):
        wq_remote(i).wait_send()
        wo_remote(i).wait_send()
    for h in range(heads):
        kv_copy(h).wait_send()

    def drain(src, carry):
        for phase in range(2):
            for h in range(CHUNKS[phase]):
                for direction, wanted, target in route(src):

                    @pl.when(wanted)
                    def _():
                        hop(phase, src, h, direction, target).wait_send()

        return carry

    lax.fori_loop(0, n, drain, 0)


def fused(n, latent, t_index, mod_table, w_qkv, w_out):
    mod_table = jnp.transpose(mod_table, (1, 0, 2))
    rows, feats = latent.shape
    depth, cols = w_qkv.shape
    depth_o, cols_o = w_out.shape
    heads = cols // (3 * HEAD_DIM)
    bf, f32 = jnp.bfloat16, jnp.float32
    dma = pltpu.SemaphoreType.DMA
    return pl.pallas_call(
        functools.partial(fused_kernel, n),
        out_shape=pltpu.VMEM((rows, feats), bf),
        in_specs=[
            pl.BlockSpec(memory_space=pltpu.HBM),
            pl.BlockSpec(memory_space=pltpu.SMEM),
            pl.BlockSpec(memory_space=pltpu.HBM),
            pl.BlockSpec(memory_space=pltpu.HBM),
            pl.BlockSpec(memory_space=pltpu.HBM),
        ],
        out_specs=pl.BlockSpec(memory_space=pltpu.VMEM),
        scratch_shapes=[
            pltpu.VMEM((n, rows, feats), bf),
            pltpu.VMEM(mod_table.shape, bf),
            pltpu.VMEM((n, 8, feats), f32),
            pltpu.VMEM((n, 2 * depth // n, cols), bf),
            pltpu.VMEM((n, 2 * depth_o // n, cols_o), bf),
            pltpu.VMEM((rows, cols), f32),
            pltpu.VMEM((2, rows, LANES), f32),
            pltpu.VMEM((rows, cols), bf),
            pltpu.VMEM((heads, rows, 2 * HEAD_DIM), bf),
            pltpu.VMEM((n, rows, heads * HEAD_DIM), bf),
            pltpu.VMEM((rows, cols_o), f32),
            dma,
            dma,
            dma((2, 3, n, max(CHUNKS))),
            dma((2, n, max(CHUNKS))),
            dma((n,)),
            dma((n,)),
            dma((n,)),
            dma((n // 2,)),
            dma((n,)),
            dma((n // 2,)),
            dma((heads,)),
            dma((heads,)),
        ],
        compiler_params=pltpu.CompilerParams(
            collective_id=0, has_side_effects=True, vmem_limit_bytes=24 * 1024 * 1024
        ),
    )(*(pltpu.with_memory_space_constraint(v, pltpu.HBM) if v.ndim > 1 else v for v in (latent, t_index, mod_table, w_qkv, w_out)))


def solution(mesh):
    in_specs = (
        P(("groups", "seq", "section"), "mp"),
        P("groups"),
        P(None, None, "mp"),
        P("section", "mp"),
        P("section", "mp"),
    )
    out_specs = P(("groups", "seq", "section"), "mp")
    n = mesh.shape["mp"]

    def body(latent, t_index, mod_table, w_qkv, w_out):
        heads = w_qkv.shape[1] // (3 * HEAD_DIM)
        fits = (
            mesh.shape["seq"] == 1
            and mesh.shape["section"] == 2
            and n % WIDE == 0
            and n > WIDE
            and heads == 2
            and latent.shape[0] <= latent.shape[1]
            and latent.shape[0] % 256 == 0
        )
        if not fits:
            return local(latent, t_index, mod_table, w_qkv, w_out)
        return fused(n, latent, t_index, mod_table, w_qkv, w_out)

    return jax.shard_map(body, mesh=mesh, in_specs=in_specs, out_specs=out_specs, check_vma=False)
```

```python
import functools
import math

import jax
import jax.numpy as jnp
from jax import lax
from jax.experimental import pallas as pl
from jax.experimental.pallas import tpu as pltpu
from jax.sharding import PartitionSpec as P

HEAD_DIM = 128
LANES = 128
WIDE = 2
PIECES = 4
MESH = pl.DeviceIdType.MESH


def layer_normed(values):
    mean_row = jnp.mean(values, axis=-1, keepdims=True)
    centred = values - mean_row
    variance = jnp.mean(centred * centred, axis=-1, keepdims=True)
    return centred * lax.rsqrt(variance + 1e-06)


def local(latent, t_index, mod_table, w_qkv, w_out):
    mod_local = lax.dynamic_index_in_dim(mod_table, t_index[0], 0, keepdims=False)
    features, mod_whole = (
        lax.all_gather(latent, "mp", axis=1, tiled=True),
        lax.all_gather(mod_local, "mp", axis=1, tiled=True),
    )
    mod_float = mod_whole.astype(jnp.float32)
    modulated = (
        layer_normed(features.astype(jnp.float32)) * (1.0 + mod_float[1]) + mod_float[0]
    ).astype(jnp.bfloat16)
    tok_rows = latent.shape[0]
    heads_dev = w_qkv.shape[1] // (3 * HEAD_DIM)
    qkv_full, out_full = (
        lax.all_gather(w_qkv, "section", axis=0, tiled=True),
        lax.all_gather(w_out, "section", axis=0, tiled=True),
    )
    projected = jnp.dot(modulated, qkv_full, preferred_element_type=jnp.float32).astype(
        jnp.bfloat16
    )
    grouped = projected.reshape(tok_rows, heads_dev, 3, HEAD_DIM)
    queries = grouped[:, :, 0]
    key_rows = grouped[:, :, 1]
    value_rows = grouped[:, :, 2]
    scale_factor = 1.0 / math.sqrt(HEAD_DIM)
    initial = (
        jnp.full((tok_rows, heads_dev), -1e30, jnp.float32),
        jnp.zeros((tok_rows, heads_dev), jnp.float32),
        jnp.zeros((tok_rows, heads_dev, HEAD_DIM), jnp.float32),
    )
    key_piece = lax.all_gather(key_rows, ("seq", "section"), axis=0, tiled=True)
    value_piece = lax.all_gather(value_rows, ("seq", "section"), axis=0, tiled=True)
    total_rows = key_piece.shape[0]
    block_rows = math.gcd(total_rows, 1024)

    def one_block(block_index, carried_block):
        running, totals, weighted = carried_block
        key_block = lax.dynamic_slice_in_dim(key_piece, block_index * block_rows, block_rows, 0)
        value_block = lax.dynamic_slice_in_dim(value_piece, block_index * block_rows, block_rows, 0)
        scores = (
            jnp.einsum("thd,khd->thk", queries, key_block, preferred_element_type=jnp.float32)
            * scale_factor
        )
        newest = jnp.maximum(running, jnp.max(scores, axis=-1))
        factor = jnp.exp(running - newest)
        weights = jnp.exp(scores - newest[..., None])
        totals = totals * factor + jnp.sum(weights, axis=-1)
        weighted = weighted * factor[..., None] + jnp.einsum(
            "thk,khd->thd",
            weights.astype(jnp.bfloat16),
            value_block,
            preferred_element_type=jnp.float32,
        )
        return (newest, totals, weighted)

    finished = lax.fori_loop(0, total_rows // block_rows, one_block, initial)
    attended = (
        (finished[2] / finished[1][..., None])
        .astype(jnp.bfloat16)
        .reshape(tok_rows, heads_dev * HEAD_DIM)
    )
    mixed_rows = jnp.dot(
        lax.all_gather(attended, "mp", axis=1, tiled=True),
        out_full,
        preferred_element_type=jnp.float32,
    )
    return (latent.astype(jnp.float32) + mod_local[2].astype(jnp.float32) * mixed_rows).astype(
        jnp.bfloat16
    )


def item_codes(deep):
    def pack(d, sign, other, far):
        return ((d * 2 + (sign < 0)) * 2 + other) * 2 + far

    both = (1, -1)
    order = [pack(0, 1, 0, 0)] + [pack(1, sign, 0, 0) for sign in both] + [pack(0, 1, 1, 0)]
    for d in range(2, deep):
        order += [pack(d, sign, 0, 0) for sign in both]
        order += [pack(d - 1, sign, 1, 0) for sign in both]
    order += [pack(deep - 1, sign, 1, 0) for sign in both]
    far = [pack(d, sign, 1, 1) for d in range(1, deep) for sign in both]
    return order, far


def fused_kernel(
    n,
    x_hbm,
    t_ref,
    mod_hbm,
    wq_hbm,
    wo_hbm,
    out_ref,
    xs,
    table,
    small,
    gate,
    wq,
    wo,
    acc,
    stat,
    proj,
    pkv,
    att,
    mixed,
    own_sem,
    table_sem,
    ssem,
    rsem,
    small_send,
    small_recv,
    wq_sem,
    wq_send,
    wo_sem,
    wo_send,
    kv_send,
    kv_recv,
    wave,
):
    me = lax.axis_index("mp")
    sec = lax.axis_index("section")
    other = 1 - sec
    deep = n // WIDE
    z, x = me // WIDE, me % WIDE
    rows, feats = x_hbm.shape
    piece_q = wq.shape[1]
    per_sec = n // 2
    piece_o = wo.shape[1]
    heads = att.shape[1]
    half = rows // 2
    above = z + 1 < deep
    below = z > 0
    at_end = jnp.logical_or(z == 0, z == deep - 1)
    beside = z * WIDE + (1 - x)
    UP, DOWN, CROSS = 0, 1, 2
    targets = (me + WIDE, me - WIDE, beside)

    barrier = pltpu.get_barrier_semaphore()
    pl.semaphore_signal(barrier, inc=1, device_id={"mp": beside}, device_id_type=MESH)
    pl.semaphore_signal(barrier, inc=1, device_id={"section": other}, device_id_type=MESH)

    @pl.when(above)
    def _():
        pl.semaphore_signal(barrier, inc=1, device_id={"mp": me + WIDE}, device_id_type=MESH)

    @pl.when(below)
    def _():
        pl.semaphore_signal(barrier, inc=1, device_id={"mp": me - WIDE}, device_id_type=MESH)

    own_copy = pltpu.make_async_copy(x_hbm, xs.at[me], own_sem)
    own_copy.start()
    table_copy = pltpu.make_async_copy(mod_hbm, table, table_sem)
    table_copy.start()

    def wq_local(i):
        p = sec * per_sec + i
        return pltpu.make_async_copy(
            wq_hbm.at[pl.ds(i * piece_q, piece_q)], wq.at[p], wq_sem.at[p]
        )

    def wo_local(i):
        return pltpu.make_async_copy(
            wo_hbm.at[pl.ds(i * piece_o, piece_o)],
            wo.at[sec * per_sec + i],
            wo_sem.at[sec * per_sec + i],
        )

    def wq_remote(i):
        p = sec * per_sec + i
        return pltpu.make_async_remote_copy(
            src_ref=wq_hbm.at[pl.ds(i * piece_q, piece_q)],
            dst_ref=wq.at[p],
            send_sem=wq_send.at[i],
            recv_sem=wq_sem.at[p],
            device_id={"section": other},
            device_id_type=MESH,
        )

    def wo_remote(i):
        p = sec * per_sec + i
        return pltpu.make_async_remote_copy(
            src_ref=wo_hbm.at[pl.ds(i * piece_o, piece_o)],
            dst_ref=wo.at[p],
            send_sem=wo_send.at[i],
            recv_sem=wo_sem.at[p],
            device_id={"section": other},
            device_id_type=MESH,
        )

    def chunk(phase, src, q):
        if phase == 0:
            part = rows // PIECES
            return xs.at[src, pl.ds(pl.multiple_of(q * part, part), part), :]
        part = rows * heads // PIECES
        return att.at[
            src, lax.rem(q, heads), pl.ds(pl.multiple_of(q // heads * part, part), part), :
        ]

    def hop(phase, src, q, direction):
        return pltpu.make_async_remote_copy(
            src_ref=chunk(phase, src, q),
            dst_ref=chunk(phase, src, q),
            send_sem=ssem.at[phase, direction, src, q],
            recv_sem=rsem.at[phase, src, q],
            device_id={"mp": targets[direction]},
            device_id_type=MESH,
        )

    def own_hop(q, direction):
        part = rows // PIECES
        return pltpu.make_async_remote_copy(
            src_ref=x_hbm.at[pl.ds(q * part, part), :],
            dst_ref=chunk(0, me, q),
            send_sem=ssem.at[0, direction, me, q],
            recv_sem=rsem.at[0, me, q],
            device_id={"mp": targets[direction]},
            device_id_type=MESH,
        )

    def outward(start):
        start(CROSS)

        @pl.when(above)
        def _():
            start(UP)

        @pl.when(below)
        def _():
            start(DOWN)

    pl.semaphore_wait(barrier, 2 + above.astype(jnp.int32) + below.astype(jnp.int32))

    def tell(which, target):
        pl.semaphore_signal(
            wave.at[which], inc=1, device_id={"mp": target}, device_id_type=MESH
        )

    @pl.when(z == 0)
    def _():
        tell(UP, me + WIDE)

    @pl.when(z == deep - 1)
    def _():
        tell(DOWN, me - WIDE)

    for q in range(PIECES - 1):
        outward(lambda direction, q=q: own_hop(q, direction).start())

    for i in range(per_sec):
        wq_local(i).start()

    own_copy.wait()
    mine = xs[me].astype(jnp.float32)
    table_copy.wait()

    def mod_row(j):
        entries = table[j].astype(jnp.float32)
        steps = lax.broadcasted_iota(jnp.int32, entries.shape, 0)
        chosen = jnp.where(steps == t_ref[0], entries, 0.0)
        return jnp.sum(chosen, axis=0, keepdims=True)

    mean_col = jnp.sum(mine, axis=1, keepdims=True) * (1.0 / feats)
    off = mine - mean_col
    m2_col = jnp.sum(off * off, axis=1, keepdims=True)
    mean_row = jnp.broadcast_to(mean_col, (rows, LANES)).T[0:1, :]
    m2_row = jnp.broadcast_to(m2_col, (rows, LANES)).T[0:1, :]
    small[me, 0:1, :] = mod_row(0)
    small[me, 1:2, :] = 1.0 + mod_row(1)
    small[me, 2:3, 0:rows] = mean_row
    small[me, 3:4, 0:rows] = m2_row
    gate[0:1, :] = mod_row(2)

    def rise():
        @pl.when(below)
        def _():
            pl.semaphore_wait(wave.at[UP], 1)

            @pl.when(above)
            def _():
                tell(UP, me + WIDE)

    def sink():
        @pl.when(above)
        def _():
            pl.semaphore_wait(wave.at[DOWN], 1)

            @pl.when(below)
            def _():
                tell(DOWN, me - WIDE)

    @pl.when(2 * z < deep)
    def _():
        rise()
        sink()

    @pl.when(2 * z >= deep)
    def _():
        sink()
        rise()

    tell(CROSS, beside)
    pl.semaphore_wait(wave.at[CROSS], 1)

    def small_copy(step):
        return pltpu.make_async_remote_copy(
            src_ref=small.at[me, pl.ds(0, 4)],
            dst_ref=small.at[me, pl.ds(0, 4)],
            send_sem=small_send.at[step],
            recv_sem=small_recv.at[me],
            device_id={"mp": lax.rem(me + step, n)},
            device_id_type=MESH,
        )

    for step in range(1, n):
        small_copy(step).start()
    outward(lambda direction: own_hop(PIECES - 1, direction).start())
    for i in range(per_sec):
        wq_remote(i).start()
    for i in range(per_sec):
        wo_local(i).start()
        wo_remote(i).start()
    acc[...] = jnp.zeros_like(acc)
    mixed[...] = jnp.zeros_like(mixed)

    near = PIECES // 2
    order, far_order = item_codes(deep)

    def lookup(table_of, j):
        found = table_of[0]
        for i in range(1, len(table_of)):
            found = jnp.where(j == i, table_of[i], found)
        return found

    def inside(sz):
        return jnp.logical_and(sz >= 0, sz < deep)

    def is_end(sz):
        return jnp.logical_or(sz == 0, sz == deep - 1)

    def item(phase, code, use_all, use_half):
        far = lax.rem(code, 2) == 1
        there = lax.rem(code // 2, 2)
        sign = 1 - 2 * lax.rem(code // 4, 2)
        d = code // 8
        sz = z + sign * d
        end = is_end(sz)
        crossed = there == 1
        src = sz * WIDE + jnp.where(crossed, 1 - x, x)
        valid = jnp.logical_and(inside(sz), jnp.logical_or(jnp.logical_not(far), end))
        cross_near = jnp.logical_and(valid, jnp.logical_and(crossed, jnp.logical_not(far)))

        @pl.when(cross_near)
        def _():
            for q in range(near):
                hop(phase, src, q, CROSS).wait_recv()

        @pl.when(jnp.logical_and(cross_near, jnp.logical_not(end)))
        def _():
            for q in range(near, PIECES):
                hop(phase, src, q, CROSS).wait_recv()

        @pl.when(jnp.logical_and(jnp.logical_and(valid, far), d == deep - 1))
        def _():
            for q in range(near, PIECES):
                hop(phase, src, q, CROSS).wait_recv()

        split = jnp.logical_and(crossed, jnp.logical_and(end, d > 0))

        @pl.when(jnp.logical_and(valid, jnp.logical_not(split)))
        def _():
            use_all(src)

        @pl.when(jnp.logical_and(valid, split))
        def _():
            use_half(src, pl.multiple_of(jnp.where(far, half, 0), half))

    def passing(phase, s, q):
        late = q >= near

        @pl.when(jnp.logical_and(jnp.logical_and(s == 1, late), at_end))
        def _():
            hop(phase, beside, q, CROSS).wait_recv()

            @pl.when(z == 0)
            def _():
                hop(phase, beside, q, UP).start()

            @pl.when(z != 0)
            def _():
                hop(phase, beside, q, DOWN).start()

        for sign, onward, has in ((1, DOWN, below), (-1, UP, above)):
            sz = z + sign * s
            src = sz * WIDE + x

            @pl.when(inside(sz))
            def _():
                hop(phase, src, q, CROSS).wait_recv()

                @pl.when(has)
                def _():
                    hop(phase, src, q, onward).start()

                @pl.when(jnp.logical_not(jnp.logical_and(late, is_end(sz))))
                def _():
                    hop(phase, src, q, CROSS).start()

        for sign, onward in ((1, DOWN), (-1, UP)):
            sz = z + sign * (s - 1)
            src = sz * WIDE + (1 - x)

            @pl.when(
                jnp.logical_and(
                    jnp.logical_and(s > 1, late), jnp.logical_and(inside(sz), is_end(sz))
                )
            )
            def _():
                hop(phase, src, q, CROSS).wait_recv()
                hop(phase, src, q, onward).start()

    def drain(phase):
        def sent(src, direction, first, last):
            for q in range(first, last):
                hop(phase, src, q, direction).wait_send()

        outward(lambda direction: sent(me, direction, 0, PIECES))

        @pl.when(z == 0)
        def _():
            sent(beside, UP, near, PIECES)

        @pl.when(z == deep - 1)
        def _():
            sent(beside, DOWN, near, PIECES)

        def one(d, carry):
            for sign, onward, has in ((1, DOWN, below), (-1, UP, above)):
                sz = z + sign * d
                src = sz * WIDE + x
                across = sz * WIDE + (1 - x)

                @pl.when(inside(sz))
                def _():
                    sent(src, CROSS, 0, near)

                    @pl.when(jnp.logical_not(is_end(sz)))
                    def _():
                        sent(src, CROSS, near, PIECES)

                    @pl.when(has)
                    def _():
                        sent(src, onward, 0, PIECES)

                    @pl.when(jnp.logical_and(has, is_end(sz)))
                    def _():
                        sent(across, onward, near, PIECES)

            return carry

        lax.fori_loop(1, deep, one, 0)

    def sweep(phase, wait_steps, prepare, use_all, use_half, between):
        steps = (deep - 1) * PIECES
        done = steps - wait_steps

        def quiet(t, carry):
            passing(phase, 1 + t // PIECES, lax.rem(t, PIECES))
            return carry

        def busy(t, carry):
            item(phase, lookup(order[:done], t - wait_steps), use_all, use_half)
            passing(phase, 1 + t // PIECES, lax.rem(t, PIECES))
            return carry

        def rest(i, carry):
            item(phase, lookup(tail, i), use_all, use_half)
            return carry

        tail = order[done:] + far_order
        lax.fori_loop(0, wait_steps, quiet, 0)
        prepare()
        lax.fori_loop(wait_steps, steps, busy, 0)
        lax.fori_loop(0, len(tail) - 2, rest, 0)
        between()
        lax.fori_loop(len(tail) - 2, len(tail), rest, 0)

    def statistics():
        for p in range(n):
            pltpu.make_async_copy(wq.at[p], wq.at[p], wq_sem.at[p]).wait()
        for step in range(1, n):
            p = lax.rem(me + step, n)
            pltpu.make_async_copy(
                small.at[p, pl.ds(0, 4)], small.at[p, pl.ds(0, 4)], small_recv.at[p]
            ).wait()
        total = jnp.zeros((1, rows), jnp.float32)
        for p in range(n):
            total = total + small[p, 2:3, 0:rows]
        grand = total * (1.0 / n)
        m2 = jnp.zeros((1, rows), jnp.float32)
        for p in range(n):
            gap = small[p, 2:3, 0:rows] - grand
            m2 = m2 + small[p, 3:4, 0:rows] + feats * (gap * gap)
        inv = lax.rsqrt(m2 * (1.0 / (n * feats)) + 1e-06)
        stat[0] = jnp.broadcast_to(grand, (LANES, rows)).T
        stat[1] = jnp.broadcast_to(inv, (LANES, rows)).T

    def project(src, start, size):
        taken = pl.ds(start, size)
        mean, rstd = stat[0, taken, :], stat[1, taken, :]
        shift_scale = small[src, 0:2, :]
        parts = []
        for c in range(feats // LANES):
            cols = slice(c * LANES, (c + 1) * LANES)
            values = xs[src, taken, cols].astype(jnp.float32)
            parts.append(
                ((values - mean) * rstd * shift_scale[1:2, cols] + shift_scale[0:1, cols]).astype(
                    jnp.bfloat16
                )
            )
        acc[taken, :] += jnp.dot(
            jnp.concatenate(parts, axis=1), wq[src], preferred_element_type=jnp.float32
        )

    sweep(
        0,
        PIECES + PIECES // 2,
        statistics,
        lambda src: project(src, 0, rows),
        lambda src, start: project(src, start, half),
        lambda: None,
    )

    def kv_copy(h):
        return pltpu.make_async_remote_copy(
            src_ref=proj.at[:, pl.ds((3 * h + 1) * HEAD_DIM, 2 * HEAD_DIM)],
            dst_ref=pkv.at[h],
            send_sem=kv_send.at[h],
            recv_sem=kv_recv.at[h],
            device_id={"section": other},
            device_id_type=MESH,
        )

    for h in range(heads):
        cols = slice((3 * h + 1) * HEAD_DIM, (3 * h + 3) * HEAD_DIM)
        proj[:, cols] = acc[:, cols].astype(jnp.bfloat16)
        kv_copy(h).start()

    factor = 1.0 / math.sqrt(HEAD_DIM)
    contract = (((1,), (1,)), ((), ()))
    part = rows * heads // PIECES
    for q in range(PIECES):
        h, taken = q % heads, pl.ds(q // heads * part, part)
        base = 3 * h * HEAD_DIM
        queries = acc[taken, base : base + HEAD_DIM].astype(jnp.bfloat16)
        own_k = proj[:, base + HEAD_DIM : base + 2 * HEAD_DIM]
        own_v = proj[:, base + 2 * HEAD_DIM : base + 3 * HEAD_DIM]
        s_own = lax.dot_general(queries, own_k, contract, preferred_element_type=jnp.float32) * factor
        if q < heads:
            kv_copy(h).wait_recv()
        far_k = pkv[h, :, 0:HEAD_DIM]
        far_v = pkv[h, :, HEAD_DIM : 2 * HEAD_DIM]
        s_far = lax.dot_general(queries, far_k, contract, preferred_element_type=jnp.float32) * factor
        top = jnp.maximum(
            jnp.max(s_own, axis=1, keepdims=True), jnp.max(s_far, axis=1, keepdims=True)
        )
        e_own = jnp.exp(s_own - top)
        e_far = jnp.exp(s_far - top)
        norm = jnp.sum(e_own, axis=1, keepdims=True) + jnp.sum(e_far, axis=1, keepdims=True)
        weighted = jnp.dot(
            e_own.astype(jnp.bfloat16), own_v, preferred_element_type=jnp.float32
        ) + jnp.dot(e_far.astype(jnp.bfloat16), far_v, preferred_element_type=jnp.float32)
        att[me, h, taken, :] = (weighted / norm).astype(jnp.bfloat16)
        outward(lambda direction, q=q: hop(1, me, q, direction).start())

    def settle():
        for p in range(n):
            pltpu.make_async_copy(wo.at[p], wo.at[p], wo_sem.at[p]).wait()
        for step in range(1, n):
            small_copy(step).wait_send()
        for i in range(per_sec):
            wq_remote(i).wait_send()
            wo_remote(i).wait_send()
        for h in range(heads):
            kv_copy(h).wait_send()
        drain(0)

    def mix(src, start, size):
        taken = pl.ds(start, size)
        joined = jnp.concatenate([att[src, h, taken, :] for h in range(heads)], axis=1)
        mixed[taken, :] += jnp.dot(joined, wo[src], preferred_element_type=jnp.float32)

    settle()
    sweep(
        1,
        PIECES,
        lambda: None,
        lambda src: mix(src, 0, rows),
        lambda src, start: mix(src, start, half),
        lambda: drain(1),
    )

    out_ref[...] = (xs[me].astype(jnp.float32) + gate[0:1, :] * mixed[...]).astype(jnp.bfloat16)


def fused(n, latent, t_index, mod_table, w_qkv, w_out):
    mod_table = jnp.transpose(mod_table, (1, 0, 2))
    rows, feats = latent.shape
    depth, cols = w_qkv.shape
    depth_o, cols_o = w_out.shape
    heads = cols // (3 * HEAD_DIM)
    bf, f32 = jnp.bfloat16, jnp.float32
    dma = pltpu.SemaphoreType.DMA
    return pl.pallas_call(
        functools.partial(fused_kernel, n),
        out_shape=pltpu.VMEM((rows, feats), bf),
        in_specs=[
            pl.BlockSpec(memory_space=pltpu.HBM),
            pl.BlockSpec(memory_space=pltpu.SMEM),
            pl.BlockSpec(memory_space=pltpu.HBM),
            pl.BlockSpec(memory_space=pltpu.HBM),
            pl.BlockSpec(memory_space=pltpu.HBM),
        ],
        out_specs=pl.BlockSpec(memory_space=pltpu.VMEM),
        scratch_shapes=[
            pltpu.VMEM((n, rows, feats), bf),
            pltpu.VMEM(mod_table.shape, bf),
            pltpu.VMEM((n, 8, feats), f32),
            pltpu.VMEM((8, feats), f32),
            pltpu.VMEM((n, 2 * depth // n, cols), bf),
            pltpu.VMEM((n, 2 * depth_o // n, cols_o), bf),
            pltpu.VMEM((rows, cols), f32),
            pltpu.VMEM((2, rows, LANES), f32),
            pltpu.VMEM((rows, cols), bf),
            pltpu.VMEM((heads, rows, 2 * HEAD_DIM), bf),
            pltpu.VMEM((n, heads, rows, HEAD_DIM), bf),
            pltpu.VMEM((rows, cols_o), f32),
            dma,
            dma,
            dma((2, 3, n, PIECES)),
            dma((2, n, PIECES)),
            dma((n,)),
            dma((n,)),
            dma((n,)),
            dma((n // 2,)),
            dma((n,)),
            dma((n // 2,)),
            dma((heads,)),
            dma((heads,)),
            pltpu.SemaphoreType.REGULAR((3,)),
        ],
        compiler_params=pltpu.CompilerParams(
            collective_id=0, has_side_effects=True, vmem_limit_bytes=24 * 1024 * 1024
        ),
    )(*(pltpu.with_memory_space_constraint(v, pltpu.HBM) if v.ndim > 1 else v for v in (latent, t_index, mod_table, w_qkv, w_out)))


def solution(mesh):
    in_specs = (
        P(("groups", "seq", "section"), "mp"),
        P("groups"),
        P(None, None, "mp"),
        P("section", "mp"),
        P("section", "mp"),
    )
    out_specs = P(("groups", "seq", "section"), "mp")
    n = mesh.shape["mp"]

    def body(latent, t_index, mod_table, w_qkv, w_out):
        heads = w_qkv.shape[1] // (3 * HEAD_DIM)
        fits = (
            mesh.shape["seq"] == 1
            and mesh.shape["section"] == 2
            and n % WIDE == 0
            and n >= 3 * WIDE
            and heads == 2
            and latent.shape[0] <= latent.shape[1]
            and latent.shape[0] % 256 == 0
        )
        if not fits:
            return local(latent, t_index, mod_table, w_qkv, w_out)
        return fused(n, latent, t_index, mod_table, w_qkv, w_out)

    return jax.shard_map(body, mesh=mesh, in_specs=in_specs, out_specs=out_specs, check_vma=False)
```

```python
import functools
import math

import jax
import jax.numpy as jnp
from jax import lax
from jax.experimental import pallas as pl
from jax.experimental.pallas import tpu as pltpu
from jax.sharding import PartitionSpec as P

HEAD_DIM = 128
LANES = 128
WIDE = 2
PIECES = 4
MESH = pl.DeviceIdType.MESH


def layer_normed(values):
    mean_row = jnp.mean(values, axis=-1, keepdims=True)
    centred = values - mean_row
    variance = jnp.mean(centred * centred, axis=-1, keepdims=True)
    return centred * lax.rsqrt(variance + 1e-06)


def local(latent, t_index, mod_table, w_qkv, w_out):
    mod_local = lax.dynamic_index_in_dim(mod_table, t_index[0], 0, keepdims=False)
    features, mod_whole = (
        lax.all_gather(latent, "mp", axis=1, tiled=True),
        lax.all_gather(mod_local, "mp", axis=1, tiled=True),
    )
    mod_float = mod_whole.astype(jnp.float32)
    modulated = (
        layer_normed(features.astype(jnp.float32)) * (1.0 + mod_float[1]) + mod_float[0]
    ).astype(jnp.bfloat16)
    tok_rows = latent.shape[0]
    heads_dev = w_qkv.shape[1] // (3 * HEAD_DIM)
    qkv_full, out_full = (
        lax.all_gather(w_qkv, "section", axis=0, tiled=True),
        lax.all_gather(w_out, "section", axis=0, tiled=True),
    )
    projected = jnp.dot(modulated, qkv_full, preferred_element_type=jnp.float32).astype(
        jnp.bfloat16
    )
    grouped = projected.reshape(tok_rows, heads_dev, 3, HEAD_DIM)
    queries = grouped[:, :, 0]
    key_rows = grouped[:, :, 1]
    value_rows = grouped[:, :, 2]
    scale_factor = 1.0 / math.sqrt(HEAD_DIM)
    initial = (
        jnp.full((tok_rows, heads_dev), -1e30, jnp.float32),
        jnp.zeros((tok_rows, heads_dev), jnp.float32),
        jnp.zeros((tok_rows, heads_dev, HEAD_DIM), jnp.float32),
    )
    key_piece = lax.all_gather(key_rows, ("seq", "section"), axis=0, tiled=True)
    value_piece = lax.all_gather(value_rows, ("seq", "section"), axis=0, tiled=True)
    total_rows = key_piece.shape[0]
    block_rows = math.gcd(total_rows, 1024)

    def one_block(block_index, carried_block):
        running, totals, weighted = carried_block
        key_block = lax.dynamic_slice_in_dim(key_piece, block_index * block_rows, block_rows, 0)
        value_block = lax.dynamic_slice_in_dim(value_piece, block_index * block_rows, block_rows, 0)
        scores = (
            jnp.einsum("thd,khd->thk", queries, key_block, preferred_element_type=jnp.float32)
            * scale_factor
        )
        newest = jnp.maximum(running, jnp.max(scores, axis=-1))
        factor = jnp.exp(running - newest)
        weights = jnp.exp(scores - newest[..., None])
        totals = totals * factor + jnp.sum(weights, axis=-1)
        weighted = weighted * factor[..., None] + jnp.einsum(
            "thk,khd->thd",
            weights.astype(jnp.bfloat16),
            value_block,
            preferred_element_type=jnp.float32,
        )
        return (newest, totals, weighted)

    finished = lax.fori_loop(0, total_rows // block_rows, one_block, initial)
    attended = (
        (finished[2] / finished[1][..., None])
        .astype(jnp.bfloat16)
        .reshape(tok_rows, heads_dev * HEAD_DIM)
    )
    mixed_rows = jnp.dot(
        lax.all_gather(attended, "mp", axis=1, tiled=True),
        out_full,
        preferred_element_type=jnp.float32,
    )
    return (latent.astype(jnp.float32) + mod_local[2].astype(jnp.float32) * mixed_rows).astype(
        jnp.bfloat16
    )


def item_codes(deep):
    def pack(d, other, far):
        return (d * 2 + other) * 2 + far

    order = [pack(0, 0, 0), pack(1, 0, 0), pack(0, 1, 0)]
    for d in range(2, deep):
        order += [pack(d, 0, 0), pack(d - 1, 1, 0)]
    order.append(pack(deep - 1, 1, 0))
    return order, [pack(d, 1, 1) for d in range(1, deep)]


def fused_kernel(
    n,
    x_hbm,
    t_ref,
    mod_hbm,
    wq_hbm,
    wo_hbm,
    out_ref,
    xs,
    table,
    mods,
    sums,
    gate,
    wq,
    wo,
    acc,
    stat,
    proj,
    pkv,
    att,
    mixed,
    own_sem,
    table_sem,
    ssem,
    rsem,
    mods_send,
    mods_recv,
    sums_send,
    sums_recv,
    wq_sem,
    wq_send,
    wo_sem,
    wo_send,
    kv_send,
    kv_recv,
    wave,
):
    me = lax.axis_index("mp")
    sec = lax.axis_index("section")
    other = 1 - sec
    deep = n // WIDE
    z, x = me // WIDE, me % WIDE
    rows, feats = x_hbm.shape
    piece_q = wq.shape[1]
    per_sec = n // 2
    piece_o = wo.shape[1]
    heads = wo.shape[1] // HEAD_DIM
    half = rows // 2
    above = z + 1 < deep
    below = z > 0
    at_end = jnp.logical_or(z == 0, z == deep - 1)
    beside = z * WIDE + (1 - x)
    UP, DOWN, CROSS = 0, 1, 2
    targets = (me + WIDE, me - WIDE, beside)

    barrier = pltpu.get_barrier_semaphore()
    pl.semaphore_signal(barrier, inc=1, device_id={"mp": beside}, device_id_type=MESH)
    pl.semaphore_signal(barrier, inc=1, device_id={"section": other}, device_id_type=MESH)

    @pl.when(above)
    def _():
        pl.semaphore_signal(barrier, inc=1, device_id={"mp": me + WIDE}, device_id_type=MESH)

    @pl.when(below)
    def _():
        pl.semaphore_signal(barrier, inc=1, device_id={"mp": me - WIDE}, device_id_type=MESH)

    own_copy = pltpu.make_async_copy(x_hbm, xs.at[pl.ds(me * rows, rows)], own_sem)
    own_copy.start()
    table_copy = pltpu.make_async_copy(mod_hbm, table, table_sem)
    table_copy.start()

    def wq_local(i):
        p = sec * per_sec + i
        return pltpu.make_async_copy(
            wq_hbm.at[pl.ds(i * piece_q, piece_q)], wq.at[p], wq_sem
        )

    def wo_local(i):
        return pltpu.make_async_copy(
            wo_hbm.at[pl.ds(i * piece_o, piece_o)],
            wo.at[sec * per_sec + i],
            wo_sem,
        )

    def wq_remote(i):
        p = sec * per_sec + i
        return pltpu.make_async_remote_copy(
            src_ref=wq_hbm.at[pl.ds(i * piece_q, piece_q)],
            dst_ref=wq.at[p],
            send_sem=wq_send,
            recv_sem=wq_sem,
            device_id={"section": other},
            device_id_type=MESH,
        )

    def wo_remote(i):
        p = sec * per_sec + i
        return pltpu.make_async_remote_copy(
            src_ref=wo_hbm.at[pl.ds(i * piece_o, piece_o)],
            dst_ref=wo.at[p],
            send_sem=wo_send,
            recv_sem=wo_sem,
            device_id={"section": other},
            device_id_type=MESH,
        )

    parts = (rows // PIECES, rows * heads // PIECES)

    def chunk(phase, src, q):
        part = parts[phase]
        if phase == 0:
            return xs.at[pl.ds(pl.multiple_of(src * rows + q * part, part), part), :]
        first = (src * heads + lax.rem(q, heads)) * rows + q // heads * part
        return att.at[pl.ds(pl.multiple_of(first, part), part), :]

    def hop(phase, src, q, direction):
        return pltpu.make_async_remote_copy(
            src_ref=chunk(phase, src, q),
            dst_ref=chunk(phase, src, q),
            send_sem=ssem.at[phase, direction],
            recv_sem=rsem.at[phase, src, q],
            device_id={"mp": targets[direction]},
            device_id_type=MESH,
        )

    near = PIECES // 2

    def own_along(phase, slot):
        q = lax.rem(slot + jnp.where(at_end, near, 0), PIECES)

        @pl.when(above)
        def _():
            hop(phase, me, q, UP).start()

        @pl.when(below)
        def _():
            hop(phase, me, q, DOWN).start()

    pl.semaphore_wait(barrier, 2 + above.astype(jnp.int32) + below.astype(jnp.int32))

    def tell(which, target):
        pl.semaphore_signal(
            wave.at[which], inc=1, device_id={"mp": target}, device_id_type=MESH
        )

    @pl.when(z == 0)
    def _():
        tell(UP, me + WIDE)

    @pl.when(z == deep - 1)
    def _():
        tell(DOWN, me - WIDE)

    def rise():
        @pl.when(below)
        def _():
            pl.semaphore_wait(wave.at[UP], 1)

            @pl.when(above)
            def _():
                tell(UP, me + WIDE)

    def sink():
        @pl.when(above)
        def _():
            pl.semaphore_wait(wave.at[DOWN], 1)

            @pl.when(below)
            def _():
                tell(DOWN, me - WIDE)

    own_copy.wait()
    for slot in range(PIECES - 1):
        hop(0, me, slot, CROSS).start()
        own_along(0, slot)

    for i in range(per_sec):
        wq_local(i).start()

    @pl.when(2 * z < deep)
    def _():
        rise()

    @pl.when(2 * z >= deep)
    def _():
        sink()

    mine = xs[pl.ds(me * rows, rows), :].astype(jnp.float32)
    table_copy.wait()

    def mod_row(j):
        entries = table[j].astype(jnp.float32)
        steps = lax.broadcasted_iota(jnp.int32, entries.shape, 0)
        chosen = jnp.where(steps == t_ref[0], entries, 0.0)
        return jnp.sum(chosen, axis=0, keepdims=True)

    mean_col = jnp.sum(mine, axis=1, keepdims=True) * (1.0 / feats)
    off = mine - mean_col
    m2_col = jnp.sum(off * off, axis=1, keepdims=True)
    mean_row = jnp.broadcast_to(mean_col, (rows, LANES)).T[0:1, :]
    m2_row = jnp.broadcast_to(m2_col, (rows, LANES)).T[0:1, :]
    mods[me, 0:2, :] = jnp.concatenate([mod_row(0), mod_row(1)], axis=0).astype(jnp.bfloat16)
    sums[me, 0:1, :] = mean_row
    sums[me, 1:2, :] = m2_row
    gate[0:1, :] = mod_row(2)

    @pl.when(2 * z < deep)
    def _():
        sink()

    @pl.when(2 * z >= deep)
    def _():
        rise()

    tell(CROSS, beside)
    pl.semaphore_wait(wave.at[CROSS], 1)

    def small_copies(step):
        return [
            pltpu.make_async_remote_copy(
                src_ref=held.at[me, pl.ds(0, 2)],
                dst_ref=held.at[me, pl.ds(0, 2)],
                send_sem=send_sem,
                recv_sem=recv_sem,
                device_id={"mp": lax.rem(me + step, n)},
                device_id_type=MESH,
            )
            for held, send_sem, recv_sem in (
                (sums, sums_send, sums_recv),
                (mods, mods_send, mods_recv),
            )
        ]

    def settled(ref, sem):
        pltpu.make_async_copy(ref, ref, sem).wait()

    for step in range(1, n):
        for copy in small_copies(step):
            copy.start()
    hop(0, me, PIECES - 1, CROSS).start()
    own_along(0, PIECES - 1)
    for i in range(per_sec):
        wq_remote(i).start()
    for i in range(per_sec):
        wo_local(i).start()
        wo_remote(i).start()
    acc[...] = jnp.zeros_like(acc)
    mixed[...] = jnp.zeros_like(mixed)

    order, far_order = item_codes(deep)

    def lookup(table_of, j):
        found = table_of[0]
        for i in range(1, len(table_of)):
            found = jnp.where(j == i, table_of[i], found)
        return found

    def inside(sz):
        return jnp.logical_and(sz >= 0, sz < deep)

    def is_end(sz):
        return jnp.logical_or(sz == 0, sz == deep - 1)

    def item(phase, code, use_all, use_half):
        far = lax.rem(code, 2) == 1
        crossed = lax.rem(code // 2, 2) == 1
        d = code // 4

        def one(i, carry):
            sz = z + (1 - 2 * i) * d
            end = is_end(sz)
            src = sz * WIDE + jnp.where(crossed, 1 - x, x)
            valid = jnp.logical_and(inside(sz), jnp.logical_or(jnp.logical_not(far), end))
            valid = jnp.logical_and(valid, jnp.logical_or(d > 0, i == 0))
            direct = jnp.logical_and(valid, jnp.logical_and(crossed, jnp.logical_not(far)))

            @pl.when(direct)
            def _():
                for q in range(near, PIECES):
                    hop(phase, src, q, CROSS).wait_recv()

            @pl.when(jnp.logical_and(direct, jnp.logical_not(end)))
            def _():
                for q in range(near):
                    hop(phase, src, q, CROSS).wait_recv()

            @pl.when(jnp.logical_and(jnp.logical_and(valid, far), d == deep - 1))
            def _():
                for q in range(near):
                    hop(phase, src, q, CROSS).wait_recv()

            split = jnp.logical_and(crossed, jnp.logical_and(end, d > 0))

            @pl.when(jnp.logical_and(valid, jnp.logical_not(split)))
            def _():
                use_all(src)

            @pl.when(jnp.logical_and(valid, split))
            def _():
                use_half(src, pl.multiple_of(jnp.where(far, 0, half), half))

            return carry

        lax.fori_loop(0, 2, one, 0)

    def passing(phase, t):
        s, slot = 1 + t // PIECES, lax.rem(t, PIECES)
        for sign, onward, has in ((1, DOWN, below), (-1, UP, above)):
            sz = z + sign * s
            src = sz * WIDE + x
            end = is_end(sz)
            q = lax.rem(slot + jnp.where(end, near, 0), PIECES)

            @pl.when(inside(sz))
            def _():
                hop(phase, src, q, CROSS).wait_recv()

                @pl.when(has)
                def _():
                    hop(phase, src, q, onward).start()

                @pl.when(jnp.logical_not(jnp.logical_and(q < near, end)))
                def _():
                    hop(phase, src, q, CROSS).start()

        first = t - 1

        @pl.when(jnp.logical_and(at_end, jnp.logical_and(first >= 0, first < near)))
        def _():
            hop(phase, beside, first, CROSS).wait_recv()

            @pl.when(z == 0)
            def _():
                hop(phase, beside, first, UP).start()

            @pl.when(z != 0)
            def _():
                hop(phase, beside, first, DOWN).start()

        for sign, onward in ((1, DOWN), (-1, UP)):
            d = deep - 1 - z if sign > 0 else z
            src = (z + sign * d) * WIDE + (1 - x)
            q = t - (PIECES * d + 2 - d)

            @pl.when(
                jnp.logical_and(
                    jnp.logical_and(d > 0, d < deep - 1), jnp.logical_and(q >= 0, q < near)
                )
            )
            def _():
                hop(phase, src, q, CROSS).wait_recv()
                hop(phase, src, q, onward).start()

    def drain(phase):
        def sent(direction, count):
            settled((xs, att)[phase].at[pl.ds(0, count * parts[phase])], ssem.at[phase, direction])

        for at in range(deep):

            @pl.when(z == at)
            def _():
                ends = at in (0, deep - 1)
                sent(CROSS, PIECES * (deep - 1) + (near if ends else 0))
                if at < deep - 1:
                    sent(UP, PIECES * (at + 1) + near)
                if at > 0:
                    sent(DOWN, PIECES * (deep - at) + near)

    def sweep(phase, wait_steps, prepare, use_all, use_half, between):
        steps = (deep - 1) * PIECES
        done = min(steps - wait_steps, len(order) - 3)

        def quiet(t, carry):
            passing(phase, t)
            return carry

        def busy(t, carry):
            item(phase, lookup(order[:done], t - wait_steps), use_all, use_half)
            passing(phase, t)
            return carry

        def rest(i, carry):
            item(phase, lookup(tail, i), use_all, use_half)
            return carry

        tail = order[done:] + far_order
        lax.fori_loop(0, wait_steps, quiet, 0)
        prepare()
        lax.fori_loop(wait_steps, wait_steps + done, busy, 0)
        lax.fori_loop(wait_steps + done, steps, quiet, 0)
        lax.fori_loop(0, len(tail) - 1, rest, 0)
        between()
        lax.fori_loop(len(tail) - 1, len(tail), rest, 0)

    def statistics():
        settled(wq, wq_sem)
        settled(sums.at[pl.ds(0, n - 1), pl.ds(0, 2)], sums_recv)
        settled(mods.at[pl.ds(0, n - 1), pl.ds(0, 2)], mods_recv)
        total = jnp.zeros((1, rows), jnp.float32)
        for p in range(n):
            total = total + sums[p, 0:1, :]
        grand = total * (1.0 / n)
        m2 = jnp.zeros((1, rows), jnp.float32)
        for p in range(n):
            gap = sums[p, 0:1, :] - grand
            m2 = m2 + sums[p, 1:2, :] + feats * (gap * gap)
        inv = lax.rsqrt(m2 * (1.0 / (n * feats)) + 1e-06)
        stat[0] = jnp.broadcast_to(grand, (LANES, rows)).T
        stat[1] = jnp.broadcast_to(inv, (LANES, rows)).T

    def project(src, start, size):
        taken = pl.ds(start, size)
        mean, rstd = stat[0, taken, :], stat[1, taken, :]
        shift = mods[src, 0:1, :].astype(jnp.float32)
        scale = 1.0 + mods[src, 1:2, :].astype(jnp.float32)
        pieces = []
        for c in range(feats // LANES):
            cols = slice(c * LANES, (c + 1) * LANES)
            values = xs[pl.ds(src * rows + start, size), cols].astype(jnp.float32)
            pieces.append(
                ((values - mean) * rstd * scale[:, cols] + shift[:, cols]).astype(jnp.bfloat16)
            )
        acc[taken, :] += jnp.dot(
            jnp.concatenate(pieces, axis=1), wq[src], preferred_element_type=jnp.float32
        )

    sweep(
        0,
        PIECES + PIECES // 2,
        statistics,
        lambda src: project(src, 0, rows),
        lambda src, start: project(src, start, half),
        lambda: None,
    )

    def kv_copy(h):
        return pltpu.make_async_remote_copy(
            src_ref=proj.at[:, pl.ds((3 * h + 1) * HEAD_DIM, 2 * HEAD_DIM)],
            dst_ref=pkv.at[h],
            send_sem=kv_send,
            recv_sem=kv_recv.at[h],
            device_id={"section": other},
            device_id_type=MESH,
        )

    for h in range(heads):
        cols = slice((3 * h + 1) * HEAD_DIM, (3 * h + 3) * HEAD_DIM)
        proj[:, cols] = acc[:, cols].astype(jnp.bfloat16)
        kv_copy(h).start()

    factor = 1.0 / math.sqrt(HEAD_DIM)
    contract = (((1,), (1,)), ((), ()))
    part = parts[1]
    for q in range(PIECES):
        h, taken = q % heads, pl.ds(q // heads * part, part)
        base = 3 * h * HEAD_DIM
        queries = acc[taken, base : base + HEAD_DIM].astype(jnp.bfloat16)
        own_k = proj[:, base + HEAD_DIM : base + 2 * HEAD_DIM]
        own_v = proj[:, base + 2 * HEAD_DIM : base + 3 * HEAD_DIM]
        s_own = lax.dot_general(queries, own_k, contract, preferred_element_type=jnp.float32) * factor
        if q < heads:
            kv_copy(h).wait_recv()
        far_k = pkv[h, :, 0:HEAD_DIM]
        far_v = pkv[h, :, HEAD_DIM : 2 * HEAD_DIM]
        s_far = lax.dot_general(queries, far_k, contract, preferred_element_type=jnp.float32) * factor
        top = jnp.maximum(
            jnp.max(s_own, axis=1, keepdims=True), jnp.max(s_far, axis=1, keepdims=True)
        )
        e_own = jnp.exp(s_own - top)
        e_far = jnp.exp(s_far - top)
        norm = jnp.sum(e_own, axis=1, keepdims=True) + jnp.sum(e_far, axis=1, keepdims=True)
        weighted = jnp.dot(
            e_own.astype(jnp.bfloat16), own_v, preferred_element_type=jnp.float32
        ) + jnp.dot(e_far.astype(jnp.bfloat16), far_v, preferred_element_type=jnp.float32)
        first = pl.multiple_of((me * heads + h) * rows + q // heads * part, part)
        att[pl.ds(first, part), :] = (weighted / norm).astype(jnp.bfloat16)
        hop(1, me, q, CROSS).start()

        @pl.when(jnp.logical_not(at_end))
        def _():
            own_along(1, q)

        if q >= near:

            @pl.when(at_end)
            def _():
                own_along(1, q - near)

    @pl.when(at_end)
    def _():
        for slot in range(near, PIECES):
            own_along(1, slot)

    def settle():
        settled(wo, wo_sem)
        settled(sums.at[pl.ds(0, n - 1), pl.ds(0, 2)], sums_send)
        settled(mods.at[pl.ds(0, n - 1), pl.ds(0, 2)], mods_send)
        settled(wq.at[pl.ds(0, per_sec)], wq_send)
        settled(wo.at[pl.ds(0, per_sec)], wo_send)
        settled(pkv, kv_send)
        drain(0)

    def mix(src, start, size):
        taken = pl.ds(start, size)
        joined = jnp.concatenate(
            [att[pl.ds((src * heads + h) * rows + start, size), :] for h in range(heads)], axis=1
        )
        mixed[taken, :] += jnp.dot(joined, wo[src], preferred_element_type=jnp.float32)

    settle()
    sweep(
        1,
        PIECES + 1,
        lambda: None,
        lambda src: mix(src, 0, rows),
        lambda src, start: mix(src, start, half),
        lambda: drain(1),
    )

    out_ref[...] = (xs[pl.ds(me * rows, rows), :].astype(jnp.float32) + gate[0:1, :] * mixed[...]).astype(jnp.bfloat16)


def fused(n, latent, t_index, mod_table, w_qkv, w_out):
    mod_table = jnp.transpose(mod_table, (1, 0, 2))
    rows, feats = latent.shape
    depth, cols = w_qkv.shape
    depth_o, cols_o = w_out.shape
    heads = cols // (3 * HEAD_DIM)
    bf, f32 = jnp.bfloat16, jnp.float32
    dma = pltpu.SemaphoreType.DMA
    return pl.pallas_call(
        functools.partial(fused_kernel, n),
        out_shape=pltpu.VMEM((rows, feats), bf),
        in_specs=[
            pl.BlockSpec(memory_space=pltpu.HBM),
            pl.BlockSpec(memory_space=pltpu.SMEM),
            pl.BlockSpec(memory_space=pltpu.HBM),
            pl.BlockSpec(memory_space=pltpu.HBM),
            pl.BlockSpec(memory_space=pltpu.HBM),
        ],
        out_specs=pl.BlockSpec(memory_space=pltpu.VMEM),
        scratch_shapes=[
            pltpu.VMEM((n * rows, feats), bf),
            pltpu.VMEM(mod_table.shape, bf),
            pltpu.VMEM((n, 16, feats), bf),
            pltpu.VMEM((n, 8, rows), f32),
            pltpu.VMEM((8, feats), f32),
            pltpu.VMEM((n, 2 * depth // n, cols), bf),
            pltpu.VMEM((n, 2 * depth_o // n, cols_o), bf),
            pltpu.VMEM((rows, cols), f32),
            pltpu.VMEM((2, rows, LANES), f32),
            pltpu.VMEM((rows, cols), bf),
            pltpu.VMEM((heads, rows, 2 * HEAD_DIM), bf),
            pltpu.VMEM((n * heads * rows, HEAD_DIM), bf),
            pltpu.VMEM((rows, cols_o), f32),
            dma,
            dma,
            dma((2, 3)),
            dma((2, n, PIECES)),
            dma,
            dma,
            dma,
            dma,
            dma,
            dma,
            dma,
            dma,
            dma,
            dma((heads,)),
            pltpu.SemaphoreType.REGULAR((3,)),
        ],
        compiler_params=pltpu.CompilerParams(
            collective_id=0, has_side_effects=True, vmem_limit_bytes=24 * 1024 * 1024
        ),
    )(*(pltpu.with_memory_space_constraint(v, pltpu.HBM) if v.ndim > 1 else v for v in (latent, t_index, mod_table, w_qkv, w_out)))


def solution(mesh):
    in_specs = (
        P(("groups", "seq", "section"), "mp"),
        P("groups"),
        P(None, None, "mp"),
        P("section", "mp"),
        P("section", "mp"),
    )
    out_specs = P(("groups", "seq", "section"), "mp")
    n = mesh.shape["mp"]

    def body(latent, t_index, mod_table, w_qkv, w_out):
        heads = w_qkv.shape[1] // (3 * HEAD_DIM)
        fits = (
            mesh.shape["seq"] == 1
            and mesh.shape["section"] == 2
            and n % WIDE == 0
            and n >= 3 * WIDE
            and heads == 2
            and latent.shape[0] <= latent.shape[1]
            and latent.shape[0] % 256 == 0
        )
        if not fits:
            return local(latent, t_index, mod_table, w_qkv, w_out)
        return fused(n, latent, t_index, mod_table, w_qkv, w_out)

    return jax.shard_map(body, mesh=mesh, in_specs=in_specs, out_specs=out_specs, check_vma=False)
```

```python
import functools
import math

import jax
import jax.numpy as jnp
from jax import lax
from jax.experimental import pallas as pl
from jax.experimental.pallas import tpu as pltpu
from jax.sharding import PartitionSpec as P

HEAD_DIM = 128
LANES = 128
WIDE = 2
PIECES = (4, 8)
MESH = pl.DeviceIdType.MESH


def layer_normed(values):
    mean_row = jnp.mean(values, axis=-1, keepdims=True)
    centred = values - mean_row
    variance = jnp.mean(centred * centred, axis=-1, keepdims=True)
    return centred * lax.rsqrt(variance + 1e-06)


def local(latent, t_index, mod_table, w_qkv, w_out):
    mod_local = lax.dynamic_index_in_dim(mod_table, t_index[0], 0, keepdims=False)
    features, mod_whole = (
        lax.all_gather(latent, "mp", axis=1, tiled=True),
        lax.all_gather(mod_local, "mp", axis=1, tiled=True),
    )
    mod_float = mod_whole.astype(jnp.float32)
    modulated = (
        layer_normed(features.astype(jnp.float32)) * (1.0 + mod_float[1]) + mod_float[0]
    ).astype(jnp.bfloat16)
    tok_rows = latent.shape[0]
    heads_dev = w_qkv.shape[1] // (3 * HEAD_DIM)
    qkv_full, out_full = (
        lax.all_gather(w_qkv, "section", axis=0, tiled=True),
        lax.all_gather(w_out, "section", axis=0, tiled=True),
    )
    projected = jnp.dot(modulated, qkv_full, preferred_element_type=jnp.float32).astype(
        jnp.bfloat16
    )
    grouped = projected.reshape(tok_rows, heads_dev, 3, HEAD_DIM)
    queries = grouped[:, :, 0]
    key_rows = grouped[:, :, 1]
    value_rows = grouped[:, :, 2]
    scale_factor = 1.0 / math.sqrt(HEAD_DIM)
    initial = (
        jnp.full((tok_rows, heads_dev), -1e30, jnp.float32),
        jnp.zeros((tok_rows, heads_dev), jnp.float32),
        jnp.zeros((tok_rows, heads_dev, HEAD_DIM), jnp.float32),
    )
    key_piece = lax.all_gather(key_rows, ("seq", "section"), axis=0, tiled=True)
    value_piece = lax.all_gather(value_rows, ("seq", "section"), axis=0, tiled=True)
    total_rows = key_piece.shape[0]
    block_rows = math.gcd(total_rows, 1024)

    def one_block(block_index, carried_block):
        running, totals, weighted = carried_block
        key_block = lax.dynamic_slice_in_dim(key_piece, block_index * block_rows, block_rows, 0)
        value_block = lax.dynamic_slice_in_dim(value_piece, block_index * block_rows, block_rows, 0)
        scores = (
            jnp.einsum("thd,khd->thk", queries, key_block, preferred_element_type=jnp.float32)
            * scale_factor
        )
        newest = jnp.maximum(running, jnp.max(scores, axis=-1))
        factor = jnp.exp(running - newest)
        weights = jnp.exp(scores - newest[..., None])
        totals = totals * factor + jnp.sum(weights, axis=-1)
        weighted = weighted * factor[..., None] + jnp.einsum(
            "thk,khd->thd",
            weights.astype(jnp.bfloat16),
            value_block,
            preferred_element_type=jnp.float32,
        )
        return (newest, totals, weighted)

    finished = lax.fori_loop(0, total_rows // block_rows, one_block, initial)
    attended = (
        (finished[2] / finished[1][..., None])
        .astype(jnp.bfloat16)
        .reshape(tok_rows, heads_dev * HEAD_DIM)
    )
    mixed_rows = jnp.dot(
        lax.all_gather(attended, "mp", axis=1, tiled=True),
        out_full,
        preferred_element_type=jnp.float32,
    )
    return (latent.astype(jnp.float32) + mod_local[2].astype(jnp.float32) * mixed_rows).astype(
        jnp.bfloat16
    )


def item_codes(deep):
    def pack(d, other, far):
        return (d * 2 + other) * 2 + far

    me, beside, idle = pack(0, 0, 0), pack(0, 1, 0), pack(deep, 0, 0)
    own = [pack(d, 0, 0) for d in range(deep)]
    cross = [pack(d, 1, 0) for d in range(deep)]
    far = [pack(d, 1, 1) for d in range(deep)]
    features = (
        [me, own[1], beside, own[2], cross[1]],
        [own[3], cross[2], cross[3], far[1], far[2], far[3]],
    )
    heads = (
        ([idle], [me]),
        ([me, own[1], beside, own[2], cross[1]], [own[1], beside, own[2], cross[1], cross[2]]),
        ([own[3], cross[2], cross[3]], [far[1], far[2], idle]),
        ([far[3]], [idle]),
    )
    return features, heads


def fused_kernel(
    n,
    x_hbm,
    t_ref,
    mod_hbm,
    wq_hbm,
    wo_hbm,
    out_ref,
    xs,
    table,
    mods,
    sums,
    gate,
    wq,
    wo,
    acc,
    stat,
    proj,
    pkv,
    att,
    mixed,
    own_sem,
    table_sem,
    ssem,
    rsem,
    mods_send,
    mods_recv,
    sums_send,
    sums_recv,
    wq_sem,
    wq_send,
    wo_sem,
    wo_send,
    kv_send,
    kv_recv,
    wave,
):
    me = lax.axis_index("mp")
    sec = lax.axis_index("section")
    other = 1 - sec
    deep = n // WIDE
    z, x = me // WIDE, me % WIDE
    rows, feats = x_hbm.shape
    piece_q = wq.shape[1]
    per_sec = n // 2
    piece_o = wo.shape[1]
    heads = wo.shape[1] // HEAD_DIM
    half = rows // 2
    above = z + 1 < deep
    below = z > 0
    at_end = jnp.logical_or(z == 0, z == deep - 1)
    beside = z * WIDE + (1 - x)
    UP, DOWN, CROSS = 0, 1, 2
    targets = (me + WIDE, me - WIDE, beside)
    into = jnp.where(2 * z < deep, 1, -1)
    inward = jnp.where(2 * z < deep, UP, DOWN)
    outer = jnp.where(2 * z < deep, DOWN, UP)
    next_in, second_in, next_out = (me + step * into * WIDE for step in (1, 2, -1))

    barrier = pltpu.get_barrier_semaphore()
    pl.semaphore_signal(barrier, inc=1, device_id={"mp": beside}, device_id_type=MESH)
    pl.semaphore_signal(barrier, inc=1, device_id={"section": other}, device_id_type=MESH)

    @pl.when(above)
    def _():
        pl.semaphore_signal(barrier, inc=1, device_id={"mp": me + WIDE}, device_id_type=MESH)

    @pl.when(below)
    def _():
        pl.semaphore_signal(barrier, inc=1, device_id={"mp": me - WIDE}, device_id_type=MESH)

    own_copy = pltpu.make_async_copy(x_hbm, xs.at[pl.ds(me * rows, rows)], own_sem)
    own_copy.start()
    table_copy = pltpu.make_async_copy(mod_hbm, table, table_sem)
    table_copy.start()

    def wq_local(i):
        p = sec * per_sec + i
        return pltpu.make_async_copy(
            wq_hbm.at[pl.ds(i * piece_q, piece_q)], wq.at[p], wq_sem
        )

    def wo_local(i):
        return pltpu.make_async_copy(
            wo_hbm.at[pl.ds(i * piece_o, piece_o)],
            wo.at[sec * per_sec + i],
            wo_sem,
        )

    def wq_remote(i):
        p = sec * per_sec + i
        return pltpu.make_async_remote_copy(
            src_ref=wq_hbm.at[pl.ds(i * piece_q, piece_q)],
            dst_ref=wq.at[p],
            send_sem=wq_send,
            recv_sem=wq_sem,
            device_id={"section": other},
            device_id_type=MESH,
        )

    def wo_remote(i):
        p = sec * per_sec + i
        return pltpu.make_async_remote_copy(
            src_ref=wo_hbm.at[pl.ds(i * piece_o, piece_o)],
            dst_ref=wo.at[p],
            send_sem=wo_send,
            recv_sem=wo_sem,
            device_id={"section": other},
            device_id_type=MESH,
        )

    parts = tuple(rows * (1, heads)[phase] // PIECES[phase] for phase in range(2))
    near_of = tuple(count // 2 for count in PIECES)
    subs = PIECES[1] // (2 * heads)

    def chunk(phase, src, q):
        part = parts[phase]
        if phase == 0:
            return xs.at[pl.ds(pl.multiple_of(src * rows + q * part, part), part), :]
        block = q // subs
        first = (src * heads + lax.rem(block, heads)) * rows
        first += (block // heads * subs + lax.rem(q, subs)) * part
        return att.at[pl.ds(pl.multiple_of(first, part), part), :]

    def hop(phase, src, q, direction, target=None):
        return pltpu.make_async_remote_copy(
            src_ref=chunk(phase, src, q),
            dst_ref=chunk(phase, src, q),
            send_sem=ssem.at[phase, direction],
            recv_sem=rsem.at[(src * PIECES[0], n * PIECES[0] + src * PIECES[1])[phase] + q],
            device_id={"mp": targets[direction] if target is None else target},
            device_id_type=MESH,
        )

    def own_along(phase, slot):
        q = lax.rem(slot + jnp.where(at_end, near_of[phase], 0), PIECES[phase])

        @pl.when(above)
        def _():
            hop(phase, me, q, UP).start()

        @pl.when(below)
        def _():
            hop(phase, me, q, DOWN).start()

    pl.semaphore_wait(barrier, 2 + above.astype(jnp.int32) + below.astype(jnp.int32))

    def tell(which, target):
        pl.semaphore_signal(
            wave.at[which], inc=1, device_id={"mp": target}, device_id_type=MESH
        )

    def rise():
        @pl.when(z > 1)
        def _():
            pl.semaphore_wait(wave.at[UP], 1)

        @pl.when(jnp.logical_and(below, above))
        def _():
            tell(UP, me + WIDE)

    def sink():
        @pl.when(z < deep - 2)
        def _():
            pl.semaphore_wait(wave.at[DOWN], 1)

        @pl.when(jnp.logical_and(below, above))
        def _():
            tell(DOWN, me - WIDE)

    own_copy.wait()
    for slot in range(PIECES[0] - 1):
        hop(0, me, slot, CROSS).start()
        own_along(0, slot)

    for i in range(per_sec):
        wq_local(i).start()

    @pl.when(2 * z < deep)
    def _():
        rise()

    @pl.when(2 * z >= deep)
    def _():
        sink()

    mine = xs[pl.ds(me * rows, rows), :].astype(jnp.float32)
    table_copy.wait()

    def mod_row(j):
        entries = table[j].astype(jnp.float32)
        steps = lax.broadcasted_iota(jnp.int32, entries.shape, 0)
        chosen = jnp.where(steps == t_ref[0], entries, 0.0)
        return jnp.sum(chosen, axis=0, keepdims=True)

    mean_col = jnp.sum(mine, axis=1, keepdims=True) * (1.0 / feats)
    off = mine - mean_col
    m2_col = jnp.sum(off * off, axis=1, keepdims=True)
    mean_row = jnp.broadcast_to(mean_col, (rows, LANES)).T[0:1, :]
    m2_row = jnp.broadcast_to(m2_col, (rows, LANES)).T[0:1, :]
    mods[me, 0:2, :] = jnp.concatenate([mod_row(0), mod_row(1)], axis=0).astype(jnp.bfloat16)
    sums[me, 0:1, :] = mean_row
    sums[me, 1:2, :] = m2_row
    gate[0:1, :] = mod_row(2)

    @pl.when(2 * z < deep)
    def _():
        sink()

    @pl.when(2 * z >= deep)
    def _():
        rise()

    tell(CROSS, beside)
    pl.semaphore_wait(wave.at[CROSS], 1)

    def small_copies(step):
        return [
            pltpu.make_async_remote_copy(
                src_ref=held.at[me, pl.ds(0, 2)],
                dst_ref=held.at[me, pl.ds(0, 2)],
                send_sem=send_sem,
                recv_sem=recv_sem,
                device_id={"mp": lax.rem(me + step, n)},
                device_id_type=MESH,
            )
            for held, send_sem, recv_sem in (
                (sums, sums_send, sums_recv),
                (mods, mods_send, mods_recv),
            )
        ]

    def settled(ref, sem):
        pltpu.make_async_copy(ref, ref, sem).wait()

    for step in range(1, n):
        for copy in small_copies(step):
            copy.start()
    hop(0, me, PIECES[0] - 1, CROSS).start()
    own_along(0, PIECES[0] - 1)
    for i in range(per_sec):
        wq_remote(i).start()
    for i in range(per_sec):
        wo_local(i).start()
        wo_remote(i).start()
    acc[...] = jnp.zeros_like(acc)
    mixed[...] = jnp.zeros_like(mixed)

    feature_items, head_items = item_codes(deep)

    def lookup(table_of, j):
        found = table_of[0]
        for i in range(1, len(table_of)):
            found = jnp.where(j == i, table_of[i], found)
        return found

    def inside(sz):
        return jnp.logical_and(sz >= 0, sz < deep)

    def is_end(sz):
        return jnp.logical_or(sz == 0, sz == deep - 1)

    def item(phase, code, use_all, use_half):
        count, near = PIECES[phase], near_of[phase]
        far = lax.rem(code, 2) == 1
        crossed = lax.rem(code // 2, 2) == 1
        d = code // 4

        def one(i, carry):
            sz = z + (1 - 2 * i) * into * d
            end = is_end(sz)
            src = sz * WIDE + jnp.where(crossed, 1 - x, x)
            valid = jnp.logical_and(inside(sz), jnp.logical_or(jnp.logical_not(far), end))
            valid = jnp.logical_and(valid, jnp.logical_or(d > 0, i == 0))
            direct = jnp.logical_and(valid, jnp.logical_and(crossed, jnp.logical_not(far)))

            @pl.when(direct)
            def _():
                for q in range(near, count):
                    hop(phase, src, q, CROSS).wait_recv()

            whole = jnp.logical_and(direct, jnp.logical_not(end))
            if phase == 1:
                whole = jnp.logical_and(whole, d > 0)

            @pl.when(whole)
            def _():
                for q in range(near):
                    hop(phase, src, q, CROSS).wait_recv()

            unseen = d == deep - 1
            if phase == 1:
                unseen = d != deep - 2

            @pl.when(jnp.logical_and(jnp.logical_and(valid, far), unseen))
            def _():
                for q in range(near):
                    hop(phase, src, q, CROSS).wait_recv()

            split = jnp.logical_and(crossed, jnp.logical_and(end, d > 0))

            @pl.when(jnp.logical_and(valid, jnp.logical_not(split)))
            def _():
                use_all(src)

            @pl.when(jnp.logical_and(valid, split))
            def _():
                use_half(src, pl.multiple_of(jnp.where(far, 0, half), half))

            return carry

        lax.fori_loop(0, jnp.where(at_end, 1, 2), one, 0)

    def passing(t):
        count, near = PIECES[0], near_of[0]
        s, slot = 1 + t // count, lax.rem(t, count)
        for sign, onward, has in ((1, DOWN, below), (-1, UP, above)):
            sz = z + sign * s
            src = sz * WIDE + x
            end = is_end(sz)
            q = lax.rem(slot + jnp.where(end, near, 0), count)

            @pl.when(inside(sz))
            def _():
                hop(0, src, q, CROSS).wait_recv()

                @pl.when(has)
                def _():
                    hop(0, src, q, onward).start()

                @pl.when(jnp.logical_not(jnp.logical_and(q < near, end)))
                def _():
                    hop(0, src, q, CROSS).start()

        first = t - 1

        @pl.when(jnp.logical_and(at_end, jnp.logical_and(first >= 0, first < near)))
        def _():
            hop(0, beside, first, CROSS).wait_recv()
            hop(0, beside, first, inward, me + into * WIDE).start()

        for sign, onward in ((1, DOWN), (-1, UP)):
            d = deep - 1 - z if sign > 0 else z
            src = (z + sign * d) * WIDE + (1 - x)
            q = t - (count * d + 2 - d)
            passed = jnp.logical_and(d > 0, d < deep - 1)

            @pl.when(jnp.logical_and(passed, jnp.logical_and(q >= 0, q < near)))
            def _():
                hop(0, src, q, CROSS).wait_recv()
                hop(0, src, q, onward).start()

    def pass_on(sz, column, turns, to=(), across=()):
        src = sz * WIDE + column
        for q in turns:
            hop(1, src, q, CROSS).wait_recv()
            for direction, target in to:
                hop(1, src, q, direction, target).start()
            if q in across:
                hop(1, src, q, CROSS).start()

    every = list(range(PIECES[1]))
    far_half, near_half = every[: near_of[1]], every[near_of[1] :]
    to_next, to_second, to_outer = (inward, next_in), (inward, second_in), (outer, next_out)

    def relay_first():
        @pl.when(at_end)
        def _():
            pass_on(z + into, x, near_half, across=near_half)
            for one in far_half:
                pass_on(z, 1 - x, [one], to=[to_second])
                pass_on(z + into, x, [one])
            for q in near_half:
                hop(1, me, q, *to_next).start()
            for q in far_half:
                hop(1, beside, q, *to_next).start()
            pass_on(z + 2 * into, x, every, across=every)

        @pl.when(jnp.logical_not(at_end))
        def _():
            pass_on(z + into, x, every, to=[to_outer], across=every)
            pass_on(z, 1 - x, far_half, to=[to_outer])
            pass_on(z - into, x, far_half, to=[to_next])
            pass_on(z + 2 * into, x, near_half, to=[to_outer], across=near_half)
            for one in far_half:
                pass_on(z + 2 * into, x, [one], to=[to_outer])
                pass_on(z + 2 * into, 1 - x, [one], to=[to_outer])
            pass_on(z - into, x, near_half, across=near_half)

    def relay_last():
        @pl.when(at_end)
        def _():
            pass_on(z + 3 * into, x, near_half + far_half, across=near_half)

    def drain(phase):
        pieces, near = PIECES[phase], near_of[phase]

        def sent(direction, count):
            settled((xs, att)[phase].at[pl.ds(0, count * parts[phase])], ssem.at[phase, direction])

        for at in range(deep):

            @pl.when(z == at)
            def _():
                ends = at in (0, deep - 1)
                if phase == 0:
                    sent(CROSS, pieces * (deep - 1) + (near if ends else 0))
                else:
                    sent(CROSS, pieces * (deep - 1))
                if phase == 0:
                    up, down = pieces * (at + 1) + near, pieces * (deep - at) + near
                elif ends:
                    up = down = pieces + near + 2 * near
                else:
                    along = (pieces + near, 3 * pieces + 2 * near)
                    up, down = along if 2 * at < deep else along[::-1]
                if at < deep - 1:
                    sent(UP, up)
                if at > 0:
                    sent(DOWN, down)

    def run(phase, items, use_all, use_half):
        end_items, middle_items = items

        def one(i, carry):
            code = jnp.where(at_end, lookup(end_items, i), lookup(middle_items, i))
            item(phase, code, use_all, use_half)
            return carry

        lax.fori_loop(0, len(end_items), one, 0)

    def gather_features(use_all, use_half):
        steps, wait_steps = (deep - 1) * PIECES[0], PIECES[0] + PIECES[0] // 2
        items, tail = feature_items

        def quiet(t, carry):
            passing(t)
            return carry

        def busy(t, carry):
            item(0, lookup(items, t - wait_steps), use_all, use_half)
            passing(t)
            return carry

        until = wait_steps + len(items)
        lax.fori_loop(0, wait_steps, quiet, 0)
        statistics()
        lax.fori_loop(wait_steps, until, busy, 0)
        lax.fori_loop(until, steps, quiet, 0)
        run(0, (tail, tail), use_all, use_half)

    def gather_heads(use_all, use_half):
        run(1, head_items[0], use_all, use_half)
        relay_first()
        run(1, head_items[1], use_all, use_half)
        relay_last()
        run(1, head_items[2], use_all, use_half)
        drain(1)
        run(1, head_items[3], use_all, use_half)

    def statistics():
        settled(wq, wq_sem)
        settled(sums.at[pl.ds(0, n - 1), pl.ds(0, 2)], sums_recv)
        settled(mods.at[pl.ds(0, n - 1), pl.ds(0, 2)], mods_recv)
        total = jnp.zeros((1, rows), jnp.float32)
        for p in range(n):
            total = total + sums[p, 0:1, :]
        grand = total * (1.0 / n)
        m2 = jnp.zeros((1, rows), jnp.float32)
        for p in range(n):
            gap = sums[p, 0:1, :] - grand
            m2 = m2 + sums[p, 1:2, :] + feats * (gap * gap)
        inv = lax.rsqrt(m2 * (1.0 / (n * feats)) + 1e-06)
        stat[0] = jnp.broadcast_to(grand, (LANES, rows)).T
        stat[1] = jnp.broadcast_to(inv, (LANES, rows)).T

    def project(src, start, size):
        taken = pl.ds(start, size)
        mean, rstd = stat[0, taken, :], stat[1, taken, :]
        shift = mods[src, 0:1, :].astype(jnp.float32)
        scale = 1.0 + mods[src, 1:2, :].astype(jnp.float32)
        pieces = []
        for c in range(feats // LANES):
            cols = slice(c * LANES, (c + 1) * LANES)
            values = xs[pl.ds(src * rows + start, size), cols].astype(jnp.float32)
            pieces.append(
                ((values - mean) * rstd * scale[:, cols] + shift[:, cols]).astype(jnp.bfloat16)
            )
        acc[taken, :] += jnp.dot(
            jnp.concatenate(pieces, axis=1), wq[src], preferred_element_type=jnp.float32
        )

    gather_features(
        lambda src: project(src, 0, rows), lambda src, start: project(src, start, half)
    )

    def kv_copy(h):
        return pltpu.make_async_remote_copy(
            src_ref=proj.at[:, pl.ds((3 * h + 1) * HEAD_DIM, 2 * HEAD_DIM)],
            dst_ref=pkv.at[h],
            send_sem=kv_send,
            recv_sem=kv_recv.at[h],
            device_id={"section": other},
            device_id_type=MESH,
        )

    for h in range(heads):
        cols = slice((3 * h + 1) * HEAD_DIM, (3 * h + 3) * HEAD_DIM)
        proj[:, cols] = acc[:, cols].astype(jnp.bfloat16)
        kv_copy(h).start()

    factor = 1.0 / math.sqrt(HEAD_DIM)
    contract = (((1,), (1,)), ((), ()))
    for block in range(2 * heads):
        h, taken = block % heads, pl.ds(block // heads * half, half)
        base = 3 * h * HEAD_DIM
        queries = acc[taken, base : base + HEAD_DIM].astype(jnp.bfloat16)
        own_k = proj[:, base + HEAD_DIM : base + 2 * HEAD_DIM]
        own_v = proj[:, base + 2 * HEAD_DIM : base + 3 * HEAD_DIM]
        s_own = lax.dot_general(queries, own_k, contract, preferred_element_type=jnp.float32) * factor
        if block < heads:
            kv_copy(h).wait_recv()
        far_k = pkv[h, :, 0:HEAD_DIM]
        far_v = pkv[h, :, HEAD_DIM : 2 * HEAD_DIM]
        s_far = lax.dot_general(queries, far_k, contract, preferred_element_type=jnp.float32) * factor
        top = jnp.maximum(
            jnp.max(s_own, axis=1, keepdims=True), jnp.max(s_far, axis=1, keepdims=True)
        )
        e_own = jnp.exp(s_own - top)
        e_far = jnp.exp(s_far - top)
        norm = jnp.sum(e_own, axis=1, keepdims=True) + jnp.sum(e_far, axis=1, keepdims=True)
        weighted = jnp.dot(
            e_own.astype(jnp.bfloat16), own_v, preferred_element_type=jnp.float32
        ) + jnp.dot(e_far.astype(jnp.bfloat16), far_v, preferred_element_type=jnp.float32)
        first = pl.multiple_of((me * heads + h) * rows + block // heads * half, half)
        att[pl.ds(first, half), :] = (weighted / norm).astype(jnp.bfloat16)
        turn = range(block * subs, (block + 1) * subs)
        for q in turn:
            hop(1, me, q, CROSS).start()

        @pl.when(jnp.logical_not(at_end))
        def _():
            for q in turn:
                hop(1, me, q, *to_next).start()
                hop(1, me, q, *to_outer).start()

        @pl.when(at_end)
        def _():
            for q in turn:
                hop(1, me, q, *(to_next if block < heads else to_second)).start()

    def settle():
        settled(wo, wo_sem)
        settled(sums.at[pl.ds(0, n - 1), pl.ds(0, 2)], sums_send)
        settled(mods.at[pl.ds(0, n - 1), pl.ds(0, 2)], mods_send)
        settled(wq.at[pl.ds(0, per_sec)], wq_send)
        settled(wo.at[pl.ds(0, per_sec)], wo_send)
        settled(pkv, kv_send)
        drain(0)

    def mix(src, start, size):
        taken = pl.ds(start, size)
        joined = jnp.concatenate(
            [att[pl.ds((src * heads + h) * rows + start, size), :] for h in range(heads)], axis=1
        )
        mixed[taken, :] += jnp.dot(joined, wo[src], preferred_element_type=jnp.float32)

    settle()
    gather_heads(lambda src: mix(src, 0, rows), lambda src, start: mix(src, start, half))

    out_ref[...] = (xs[pl.ds(me * rows, rows), :].astype(jnp.float32) + gate[0:1, :] * mixed[...]).astype(jnp.bfloat16)


def fused(n, latent, t_index, mod_table, w_qkv, w_out):
    mod_table = jnp.transpose(mod_table, (1, 0, 2))
    rows, feats = latent.shape
    depth, cols = w_qkv.shape
    depth_o, cols_o = w_out.shape
    heads = cols // (3 * HEAD_DIM)
    bf, f32 = jnp.bfloat16, jnp.float32
    dma = pltpu.SemaphoreType.DMA
    return pl.pallas_call(
        functools.partial(fused_kernel, n),
        out_shape=pltpu.VMEM((rows, feats), bf),
        in_specs=[
            pl.BlockSpec(memory_space=pltpu.HBM),
            pl.BlockSpec(memory_space=pltpu.SMEM),
            pl.BlockSpec(memory_space=pltpu.HBM),
            pl.BlockSpec(memory_space=pltpu.HBM),
            pl.BlockSpec(memory_space=pltpu.HBM),
        ],
        out_specs=pl.BlockSpec(memory_space=pltpu.VMEM),
        scratch_shapes=[
            pltpu.VMEM((n * rows, feats), bf),
            pltpu.VMEM(mod_table.shape, bf),
            pltpu.VMEM((n, 16, feats), bf),
            pltpu.VMEM((n, 8, rows), f32),
            pltpu.VMEM((8, feats), f32),
            pltpu.VMEM((n, 2 * depth // n, cols), bf),
            pltpu.VMEM((n, 2 * depth_o // n, cols_o), bf),
            pltpu.VMEM((rows, cols), f32),
            pltpu.VMEM((2, rows, LANES), f32),
            pltpu.VMEM((rows, cols), bf),
            pltpu.VMEM((heads, rows, 2 * HEAD_DIM), bf),
            pltpu.VMEM((n * heads * rows, HEAD_DIM), bf),
            pltpu.VMEM((rows, cols_o), f32),
            dma,
            dma,
            dma((2, 3)),
            dma((n * sum(PIECES),)),
            dma,
            dma,
            dma,
            dma,
            dma,
            dma,
            dma,
            dma,
            dma,
            dma((heads,)),
            pltpu.SemaphoreType.REGULAR((3,)),
        ],
        compiler_params=pltpu.CompilerParams(
            collective_id=0, has_side_effects=True, vmem_limit_bytes=24 * 1024 * 1024
        ),
    )(*(pltpu.with_memory_space_constraint(v, pltpu.HBM) if v.ndim > 1 else v for v in (latent, t_index, mod_table, w_qkv, w_out)))


def solution(mesh):
    in_specs = (
        P(("groups", "seq", "section"), "mp"),
        P("groups"),
        P(None, None, "mp"),
        P("section", "mp"),
        P("section", "mp"),
    )
    out_specs = P(("groups", "seq", "section"), "mp")
    n = mesh.shape["mp"]

    def body(latent, t_index, mod_table, w_qkv, w_out):
        heads = w_qkv.shape[1] // (3 * HEAD_DIM)
        fits = (
            mesh.shape["seq"] == 1
            and mesh.shape["section"] == 2
            and n % WIDE == 0
            and n == 4 * WIDE
            and heads == 2
            and latent.shape[0] <= latent.shape[1]
            and latent.shape[0] % 256 == 0
        )
        if not fits:
            return local(latent, t_index, mod_table, w_qkv, w_out)
        return fused(n, latent, t_index, mod_table, w_qkv, w_out)

    return jax.shard_map(body, mesh=mesh, in_specs=in_specs, out_specs=out_specs, check_vma=False)
```

```python
import functools
import math

import jax
import jax.numpy as jnp
from jax import lax
from jax.experimental import pallas as pl
from jax.experimental.pallas import tpu as pltpu
from jax.sharding import PartitionSpec as P

HEAD_DIM = 128
LANES = 128
WIDE = 2
PIECES = (4, 8)
MESH = pl.DeviceIdType.MESH


def layer_normed(values):
    mean_row = jnp.mean(values, axis=-1, keepdims=True)
    centred = values - mean_row
    variance = jnp.mean(centred * centred, axis=-1, keepdims=True)
    return centred * lax.rsqrt(variance + 1e-06)


def local(latent, t_index, mod_table, w_qkv, w_out):
    mod_local = lax.dynamic_index_in_dim(mod_table, t_index[0], 0, keepdims=False)
    features, mod_whole = (
        lax.all_gather(latent, "mp", axis=1, tiled=True),
        lax.all_gather(mod_local, "mp", axis=1, tiled=True),
    )
    mod_float = mod_whole.astype(jnp.float32)
    modulated = (
        layer_normed(features.astype(jnp.float32)) * (1.0 + mod_float[1]) + mod_float[0]
    ).astype(jnp.bfloat16)
    tok_rows = latent.shape[0]
    heads_dev = w_qkv.shape[1] // (3 * HEAD_DIM)
    qkv_full, out_full = (
        lax.all_gather(w_qkv, "section", axis=0, tiled=True),
        lax.all_gather(w_out, "section", axis=0, tiled=True),
    )
    projected = jnp.dot(modulated, qkv_full, preferred_element_type=jnp.float32).astype(
        jnp.bfloat16
    )
    grouped = projected.reshape(tok_rows, heads_dev, 3, HEAD_DIM)
    queries = grouped[:, :, 0]
    key_rows = grouped[:, :, 1]
    value_rows = grouped[:, :, 2]
    scale_factor = 1.0 / math.sqrt(HEAD_DIM)
    initial = (
        jnp.full((tok_rows, heads_dev), -1e30, jnp.float32),
        jnp.zeros((tok_rows, heads_dev), jnp.float32),
        jnp.zeros((tok_rows, heads_dev, HEAD_DIM), jnp.float32),
    )
    key_piece = lax.all_gather(key_rows, ("seq", "section"), axis=0, tiled=True)
    value_piece = lax.all_gather(value_rows, ("seq", "section"), axis=0, tiled=True)
    total_rows = key_piece.shape[0]
    block_rows = math.gcd(total_rows, 1024)

    def one_block(block_index, carried_block):
        running, totals, weighted = carried_block
        key_block = lax.dynamic_slice_in_dim(key_piece, block_index * block_rows, block_rows, 0)
        value_block = lax.dynamic_slice_in_dim(value_piece, block_index * block_rows, block_rows, 0)
        scores = (
            jnp.einsum("thd,khd->thk", queries, key_block, preferred_element_type=jnp.float32)
            * scale_factor
        )
        newest = jnp.maximum(running, jnp.max(scores, axis=-1))
        factor = jnp.exp(running - newest)
        weights = jnp.exp(scores - newest[..., None])
        totals = totals * factor + jnp.sum(weights, axis=-1)
        weighted = weighted * factor[..., None] + jnp.einsum(
            "thk,khd->thd",
            weights.astype(jnp.bfloat16),
            value_block,
            preferred_element_type=jnp.float32,
        )
        return (newest, totals, weighted)

    finished = lax.fori_loop(0, total_rows // block_rows, one_block, initial)
    attended = (
        (finished[2] / finished[1][..., None])
        .astype(jnp.bfloat16)
        .reshape(tok_rows, heads_dev * HEAD_DIM)
    )
    mixed_rows = jnp.dot(
        lax.all_gather(attended, "mp", axis=1, tiled=True),
        out_full,
        preferred_element_type=jnp.float32,
    )
    return (latent.astype(jnp.float32) + mod_local[2].astype(jnp.float32) * mixed_rows).astype(
        jnp.bfloat16
    )


def item_codes(deep):
    def pack(d, other, far):
        return (d * 2 + other) * 2 + far

    me, beside, idle = pack(0, 0, 0), pack(0, 1, 0), pack(deep, 0, 0)
    own = [pack(d, 0, 0) for d in range(deep)]
    cross = [pack(d, 1, 0) for d in range(deep)]
    far = [pack(d, 1, 1) for d in range(deep)]
    features = (
        [me, own[1], beside, own[2], cross[1]],
        [own[3], cross[2], cross[3], far[1], far[2], far[3]],
    )
    heads = (
        ([idle], [me]),
        ([me, own[1], beside, own[2], cross[1]], [own[1], beside, own[2], cross[1], cross[2]]),
        ([cross[2], own[3], pack(3, 0, 1), far[3]], [far[1], far[2], idle, idle]),
        ([cross[3]], [idle]),
    )
    return features, heads


def fused_kernel(
    n,
    x_hbm,
    t_ref,
    mod_hbm,
    wq_hbm,
    wo_hbm,
    out_ref,
    xs,
    table,
    mods,
    sums,
    gate,
    wq,
    wo,
    acc,
    stat,
    proj,
    pkv,
    att,
    mixed,
    own_sem,
    table_sem,
    ssem,
    rsem,
    mods_send,
    mods_recv,
    sums_send,
    sums_recv,
    wq_sem,
    wq_send,
    wo_sem,
    wo_send,
    kv_send,
    kv_recv,
    wave,
):
    me = lax.axis_index("mp")
    sec = lax.axis_index("section")
    other = 1 - sec
    deep = n // WIDE
    z, x = me // WIDE, me % WIDE
    rows, feats = x_hbm.shape
    piece_q = wq.shape[1]
    per_sec = n // 2
    piece_o = wo.shape[1]
    heads = wo.shape[1] // HEAD_DIM
    half = rows // 2
    above = z + 1 < deep
    below = z > 0
    at_end = jnp.logical_or(z == 0, z == deep - 1)
    beside = z * WIDE + (1 - x)
    UP, DOWN, CROSS = 0, 1, 2
    targets = (me + WIDE, me - WIDE, beside)
    into = jnp.where(2 * z < deep, 1, -1)
    inward = jnp.where(2 * z < deep, UP, DOWN)
    outer = jnp.where(2 * z < deep, DOWN, UP)
    next_in, second_in, next_out = (me + step * into * WIDE for step in (1, 2, -1))

    barrier = pltpu.get_barrier_semaphore()
    pl.semaphore_signal(barrier, inc=1, device_id={"mp": beside}, device_id_type=MESH)
    pl.semaphore_signal(barrier, inc=1, device_id={"section": other}, device_id_type=MESH)

    @pl.when(above)
    def _():
        pl.semaphore_signal(barrier, inc=1, device_id={"mp": me + WIDE}, device_id_type=MESH)

    @pl.when(below)
    def _():
        pl.semaphore_signal(barrier, inc=1, device_id={"mp": me - WIDE}, device_id_type=MESH)

    def own_copy(q):
        part = rows // PIECES[0]
        return pltpu.make_async_copy(
            x_hbm.at[pl.ds(q * part, part)],
            xs.at[pl.ds(pl.multiple_of(me * rows + q * part, part), part)],
            own_sem.at[q],
        )

    for q in range(PIECES[0]):
        own_copy(q).start()
    table_copy = pltpu.make_async_copy(mod_hbm, table, table_sem)
    table_copy.start()

    def wq_local(i):
        p = sec * per_sec + i
        return pltpu.make_async_copy(
            wq_hbm.at[pl.ds(i * piece_q, piece_q)], wq.at[p], wq_sem
        )

    def wo_local(i):
        return pltpu.make_async_copy(
            wo_hbm.at[pl.ds(i * piece_o, piece_o)],
            wo.at[sec * per_sec + i],
            wo_sem,
        )

    def wq_remote(i):
        p = sec * per_sec + i
        return pltpu.make_async_remote_copy(
            src_ref=wq_hbm.at[pl.ds(i * piece_q, piece_q)],
            dst_ref=wq.at[p],
            send_sem=wq_send,
            recv_sem=wq_sem,
            device_id={"section": other},
            device_id_type=MESH,
        )

    def wo_remote(i):
        p = sec * per_sec + i
        return pltpu.make_async_remote_copy(
            src_ref=wo_hbm.at[pl.ds(i * piece_o, piece_o)],
            dst_ref=wo.at[p],
            send_sem=wo_send,
            recv_sem=wo_sem,
            device_id={"section": other},
            device_id_type=MESH,
        )

    parts = tuple(rows * (1, heads)[phase] // PIECES[phase] for phase in range(2))
    near_of = tuple(count // 2 for count in PIECES)
    subs = PIECES[1] // (2 * heads)

    def chunk(phase, src, q):
        part = parts[phase]
        if phase == 0:
            return xs.at[pl.ds(pl.multiple_of(src * rows + q * part, part), part), :]
        block = q // subs
        first = (src * heads + lax.rem(block, heads)) * rows
        first += (block // heads * subs + lax.rem(q, subs)) * part
        return att.at[pl.ds(pl.multiple_of(first, part), part), :]

    def hop(phase, src, q, direction, target=None):
        return pltpu.make_async_remote_copy(
            src_ref=chunk(phase, src, q),
            dst_ref=chunk(phase, src, q),
            send_sem=ssem.at[phase, direction],
            recv_sem=rsem.at[(src * PIECES[0], n * PIECES[0] + src * PIECES[1])[phase] + q],
            device_id={"mp": targets[direction] if target is None else target},
            device_id_type=MESH,
        )

    def own_along(phase, slot):
        q = lax.rem(slot + jnp.where(at_end, near_of[phase], 0), PIECES[phase])

        @pl.when(above)
        def _():
            hop(phase, me, q, UP).start()

        @pl.when(below)
        def _():
            hop(phase, me, q, DOWN).start()

    pl.semaphore_wait(barrier, 2 + above.astype(jnp.int32) + below.astype(jnp.int32))

    def tell(which, target):
        pl.semaphore_signal(
            wave.at[which], inc=1, device_id={"mp": target}, device_id_type=MESH
        )

    def rise():
        @pl.when(z > 1)
        def _():
            pl.semaphore_wait(wave.at[UP], 1)

        @pl.when(jnp.logical_and(below, above))
        def _():
            tell(UP, me + WIDE)

    def sink():
        @pl.when(z < deep - 2)
        def _():
            pl.semaphore_wait(wave.at[DOWN], 1)

        @pl.when(jnp.logical_and(below, above))
        def _():
            tell(DOWN, me - WIDE)

    for slot in range(PIECES[0] - 1):
        if slot < near_of[0]:
            own_copy(slot).wait()
            own_copy(slot + near_of[0]).wait()
        hop(0, me, slot, CROSS).start()
        own_along(0, slot)

    for i in range(per_sec):
        wq_local(i).start()

    @pl.when(2 * z < deep)
    def _():
        rise()

    @pl.when(2 * z >= deep)
    def _():
        sink()

    mine = xs[pl.ds(me * rows, rows), :].astype(jnp.float32)
    table_copy.wait()

    def mod_row(j):
        entries = table[j].astype(jnp.float32)
        steps = lax.broadcasted_iota(jnp.int32, entries.shape, 0)
        chosen = jnp.where(steps == t_ref[0], entries, 0.0)
        return jnp.sum(chosen, axis=0, keepdims=True)

    mean_col = jnp.sum(mine, axis=1, keepdims=True) * (1.0 / feats)
    off = mine - mean_col
    m2_col = jnp.sum(off * off, axis=1, keepdims=True)
    mean_row = jnp.broadcast_to(mean_col, (rows, LANES)).T[0:1, :]
    m2_row = jnp.broadcast_to(m2_col, (rows, LANES)).T[0:1, :]
    mods[me, 0:2, :] = jnp.concatenate([mod_row(0), mod_row(1)], axis=0).astype(jnp.bfloat16)
    sums[me, 0:1, :] = mean_row
    sums[me, 1:2, :] = m2_row
    gate[0:1, :] = mod_row(2)

    @pl.when(2 * z < deep)
    def _():
        sink()

    @pl.when(2 * z >= deep)
    def _():
        rise()

    tell(CROSS, beside)
    pl.semaphore_wait(wave.at[CROSS], 1)

    def small_copies(step):
        return [
            pltpu.make_async_remote_copy(
                src_ref=held.at[me, pl.ds(0, 2)],
                dst_ref=held.at[me, pl.ds(0, 2)],
                send_sem=send_sem,
                recv_sem=recv_sem,
                device_id={"mp": lax.rem(me + step, n)},
                device_id_type=MESH,
            )
            for held, send_sem, recv_sem in (
                (sums, sums_send, sums_recv),
                (mods, mods_send, mods_recv),
            )
        ]

    def settled(ref, sem):
        pltpu.make_async_copy(ref, ref, sem).wait()

    for step in range(1, n):
        for copy in small_copies(step):
            copy.start()
    hop(0, me, PIECES[0] - 1, CROSS).start()
    own_along(0, PIECES[0] - 1)
    for i in range(per_sec):
        wq_remote(i).start()
    for i in range(per_sec):
        wo_local(i).start()
        wo_remote(i).start()
    acc[...] = jnp.zeros_like(acc)
    mixed[...] = jnp.zeros_like(mixed)

    feature_items, head_items = item_codes(deep)

    def lookup(table_of, j):
        found = table_of[0]
        for i in range(1, len(table_of)):
            found = jnp.where(j == i, table_of[i], found)
        return found

    def inside(sz):
        return jnp.logical_and(sz >= 0, sz < deep)

    def is_end(sz):
        return jnp.logical_or(sz == 0, sz == deep - 1)

    def item(phase, code, use_all, use_half):
        count, near = PIECES[phase], near_of[phase]
        far = lax.rem(code, 2) == 1
        crossed = lax.rem(code // 2, 2) == 1
        d = code // 4

        def one(i, carry):
            sz = z + (1 - 2 * i) * into * d
            end = is_end(sz)
            src = sz * WIDE + jnp.where(crossed, 1 - x, x)
            valid = jnp.logical_and(inside(sz), jnp.logical_or(jnp.logical_not(far), end))
            valid = jnp.logical_and(valid, jnp.logical_or(d > 0, i == 0))
            direct = jnp.logical_and(valid, jnp.logical_and(crossed, jnp.logical_not(far)))

            @pl.when(direct)
            def _():
                for q in range(near, count):
                    hop(phase, src, q, CROSS).wait_recv()

            whole = jnp.logical_and(direct, jnp.logical_not(end))
            if phase == 1:
                whole = jnp.logical_and(whole, d > 0)

            @pl.when(whole)
            def _():
                for q in range(near):
                    hop(phase, src, q, CROSS).wait_recv()

            unseen = d == deep - 1
            if phase == 1:
                unseen = d != deep - 2

            @pl.when(jnp.logical_and(jnp.logical_and(valid, far), unseen))
            def _():
                for q in range(near):
                    hop(phase, src, q, CROSS).wait_recv()

            halved = crossed
            if phase == 1:
                halved = jnp.logical_or(crossed, d == deep - 1)
            split = jnp.logical_and(halved, jnp.logical_and(end, d > 0))

            @pl.when(jnp.logical_and(valid, jnp.logical_not(split)))
            def _():
                use_all(src)

            @pl.when(jnp.logical_and(valid, split))
            def _():
                use_half(src, pl.multiple_of(jnp.where(far, 0, half), half))

            return carry

        lax.fori_loop(0, jnp.where(at_end, 1, 2), one, 0)

    def passing(t):
        count, near = PIECES[0], near_of[0]
        s, slot = 1 + t // count, lax.rem(t, count)
        for sign, onward, has in ((1, DOWN, below), (-1, UP, above)):
            sz = z + sign * s
            src = sz * WIDE + x
            end = is_end(sz)
            q = lax.rem(slot + jnp.where(end, near, 0), count)

            @pl.when(inside(sz))
            def _():
                hop(0, src, q, CROSS).wait_recv()

                @pl.when(has)
                def _():
                    hop(0, src, q, onward).start()

                @pl.when(jnp.logical_not(jnp.logical_and(q < near, end)))
                def _():
                    hop(0, src, q, CROSS).start()

        first = t - 1

        @pl.when(jnp.logical_and(at_end, jnp.logical_and(first >= 0, first < near)))
        def _():
            hop(0, beside, first, CROSS).wait_recv()
            hop(0, beside, first, inward, me + into * WIDE).start()

        for sign, onward in ((1, DOWN), (-1, UP)):
            d = deep - 1 - z if sign > 0 else z
            src = (z + sign * d) * WIDE + (1 - x)
            q = t - (count * d + 2 - d)
            passed = jnp.logical_and(d > 0, d < deep - 1)

            @pl.when(jnp.logical_and(passed, jnp.logical_and(q >= 0, q < near)))
            def _():
                hop(0, src, q, CROSS).wait_recv()
                hop(0, src, q, onward).start()

    def pass_on(sz, column, turns, to=(), across=()):
        src = sz * WIDE + column
        for q in turns:
            hop(1, src, q, CROSS).wait_recv()
            for direction, target in to:
                hop(1, src, q, direction, target).start()
            if q in across:
                hop(1, src, q, CROSS).start()

    every = list(range(PIECES[1]))
    far_half, near_half = every[: near_of[1]], every[near_of[1] :]
    to_next, to_second, to_outer = (inward, next_in), (inward, second_in), (outer, next_out)

    def relay_first():
        @pl.when(at_end)
        def _():
            pass_on(z + into, x, near_half, across=near_half)
            for one in far_half:
                pass_on(z, 1 - x, [one], to=[to_second])
                pass_on(z + into, x, [one])
            for q in near_half:
                hop(1, me, q, *to_next).start()
            for q in far_half:
                hop(1, beside, q, *to_next).start()
            pass_on(z + 2 * into, x, every, across=every)

        @pl.when(jnp.logical_not(at_end))
        def _():
            pass_on(z + into, x, every, to=[to_outer], across=every)
            pass_on(z, 1 - x, far_half, to=[to_outer])
            pass_on(z - into, x, far_half, to=[to_next])
            pass_on(z + 2 * into, x, near_half, to=[to_outer], across=near_half)
            for one in far_half:
                pass_on(z + 2 * into, x, [one], to=[to_outer])
                pass_on(z + 2 * into, 1 - x, [one], to=[to_outer])
            pass_on(z - into, x, near_half, across=near_half)

    def relay_last():
        @pl.when(at_end)
        def _():
            pass_on(z + 3 * into, x, near_half, across=near_half)

    def drain(phase):
        pieces, near = PIECES[phase], near_of[phase]

        def sent(direction, count):
            settled((xs, att)[phase].at[pl.ds(0, count * parts[phase])], ssem.at[phase, direction])

        for at in range(deep):

            @pl.when(z == at)
            def _():
                ends = at in (0, deep - 1)
                if phase == 0:
                    sent(CROSS, pieces * (deep - 1) + (near if ends else 0))
                else:
                    sent(CROSS, pieces * (deep - 1))
                if phase == 0:
                    up, down = pieces * (at + 1) + near, pieces * (deep - at) + near
                elif ends:
                    up = down = pieces + near + 2 * near
                else:
                    along = (pieces + near, 3 * pieces + 2 * near)
                    up, down = along if 2 * at < deep else along[::-1]
                if at < deep - 1:
                    sent(UP, up)
                if at > 0:
                    sent(DOWN, down)

    def run(phase, items, use_all, use_half):
        end_items, middle_items = items

        def one(i, carry):
            code = jnp.where(at_end, lookup(end_items, i), lookup(middle_items, i))
            item(phase, code, use_all, use_half)
            return carry

        lax.fori_loop(0, len(end_items), one, 0)

    def gather_features(use_all, use_half):
        steps, wait_steps = (deep - 1) * PIECES[0], PIECES[0] + PIECES[0] // 2
        items, tail = feature_items

        def quiet(t, carry):
            passing(t)
            return carry

        def busy(t, carry):
            item(0, lookup(items, t - wait_steps), use_all, use_half)
            passing(t)
            return carry

        until = wait_steps + len(items)
        lax.fori_loop(0, wait_steps, quiet, 0)
        statistics()
        lax.fori_loop(wait_steps, until, busy, 0)
        lax.fori_loop(until, steps, quiet, 0)
        run(0, (tail, tail), use_all, use_half)

    def gather_heads(use_all, use_half):
        run(1, head_items[0], use_all, use_half)
        relay_first()
        run(1, head_items[1], use_all, use_half)
        relay_last()
        run(1, head_items[2], use_all, use_half)
        drain(1)
        run(1, head_items[3], use_all, use_half)

    def statistics():
        settled(wq, wq_sem)
        settled(sums.at[pl.ds(0, n - 1), pl.ds(0, 2)], sums_recv)
        settled(mods.at[pl.ds(0, n - 1), pl.ds(0, 2)], mods_recv)
        total = jnp.zeros((1, rows), jnp.float32)
        for p in range(n):
            total = total + sums[p, 0:1, :]
        grand = total * (1.0 / n)
        m2 = jnp.zeros((1, rows), jnp.float32)
        for p in range(n):
            gap = sums[p, 0:1, :] - grand
            m2 = m2 + sums[p, 1:2, :] + feats * (gap * gap)
        inv = lax.rsqrt(m2 * (1.0 / (n * feats)) + 1e-06)
        stat[0] = jnp.broadcast_to(grand, (LANES, rows)).T
        stat[1] = jnp.broadcast_to(inv, (LANES, rows)).T

    def project(src, start, size):
        taken = pl.ds(start, size)
        mean, rstd = stat[0, taken, :], stat[1, taken, :]
        shift = mods[src, 0:1, :].astype(jnp.float32)
        scale = 1.0 + mods[src, 1:2, :].astype(jnp.float32)
        pieces = []
        for c in range(feats // LANES):
            cols = slice(c * LANES, (c + 1) * LANES)
            values = xs[pl.ds(src * rows + start, size), cols].astype(jnp.float32)
            pieces.append(
                ((values - mean) * rstd * scale[:, cols] + shift[:, cols]).astype(jnp.bfloat16)
            )
        acc[taken, :] += jnp.dot(
            jnp.concatenate(pieces, axis=1), wq[src], preferred_element_type=jnp.float32
        )

    gather_features(
        lambda src: project(src, 0, rows), lambda src, start: project(src, start, half)
    )

    def kv_copy(h):
        return pltpu.make_async_remote_copy(
            src_ref=proj.at[:, pl.ds((3 * h + 1) * HEAD_DIM, 2 * HEAD_DIM)],
            dst_ref=pkv.at[h],
            send_sem=kv_send,
            recv_sem=kv_recv.at[h],
            device_id={"section": other},
            device_id_type=MESH,
        )

    for h in range(heads):
        cols = slice((3 * h + 1) * HEAD_DIM, (3 * h + 3) * HEAD_DIM)
        proj[:, cols] = acc[:, cols].astype(jnp.bfloat16)
        kv_copy(h).start()

    factor = math.log2(math.e) / math.sqrt(HEAD_DIM)
    contract = (((1,), (1,)), ((), ()))
    def attend(taken):
        raw, tops, sides = [], [], []
        for h in range(heads):
            base = 3 * h * HEAD_DIM
            queries = acc[taken, base : base + HEAD_DIM].astype(jnp.bfloat16)
            own_k = proj[:, base + HEAD_DIM : base + 2 * HEAD_DIM]
            far_k = pkv[h, :, 0:HEAD_DIM]
            raw.append(
                [
                    lax.dot_general(queries, keys, contract, preferred_element_type=jnp.float32)
                    for keys in (own_k, far_k)
                ]
            )
        for own_s, far_s in raw:
            tops.append(
                jnp.maximum(
                    jnp.max(own_s, axis=1, keepdims=True), jnp.max(far_s, axis=1, keepdims=True)
                )
            )
        for pair, top in zip(raw, tops):
            sides.append([jnp.exp2((scores - top) * factor) for scores in pair])
        results = []
        for h, (e_own, e_far) in enumerate(sides):
            base = 3 * h * HEAD_DIM
            own_v = proj[:, base + 2 * HEAD_DIM : base + 3 * HEAD_DIM]
            far_v = pkv[h, :, HEAD_DIM : 2 * HEAD_DIM]
            norm = jnp.sum(e_own, axis=1, keepdims=True) + jnp.sum(e_far, axis=1, keepdims=True)
            weighted = jnp.dot(
                e_own.astype(jnp.bfloat16), own_v, preferred_element_type=jnp.float32
            ) + jnp.dot(e_far.astype(jnp.bfloat16), far_v, preferred_element_type=jnp.float32)
            results.append((weighted / norm).astype(jnp.bfloat16))
        return results

    for h in range(heads):
        kv_copy(h).wait_recv()
    for turn, first_half in ((far_half, True), (near_half, False)):
        start = 0 if first_half else half
        for h, result in enumerate(attend(pl.ds(start, half))):
            att[pl.ds(pl.multiple_of((me * heads + h) * rows + start, half), half), :] = result
        for q in turn:
            hop(1, me, q, CROSS).start()

        @pl.when(jnp.logical_not(at_end))
        def _():
            for q in turn:
                hop(1, me, q, *to_next).start()
                hop(1, me, q, *to_outer).start()

        @pl.when(at_end)
        def _():
            for q in turn:
                hop(1, me, q, *(to_next if first_half else to_second)).start()

    def settle():
        settled(wo, wo_sem)
        settled(sums.at[pl.ds(0, n - 1), pl.ds(0, 2)], sums_send)
        settled(mods.at[pl.ds(0, n - 1), pl.ds(0, 2)], mods_send)
        settled(wq.at[pl.ds(0, per_sec)], wq_send)
        settled(wo.at[pl.ds(0, per_sec)], wo_send)
        settled(pkv, kv_send)
        drain(0)

    def mix(src, start, size):
        taken = pl.ds(start, size)
        joined = jnp.concatenate(
            [att[pl.ds((src * heads + h) * rows + start, size), :] for h in range(heads)], axis=1
        )
        mixed[taken, :] += jnp.dot(joined, wo[src], preferred_element_type=jnp.float32)

    settle()
    gather_heads(lambda src: mix(src, 0, rows), lambda src, start: mix(src, start, half))

    out_ref[...] = (xs[pl.ds(me * rows, rows), :].astype(jnp.float32) + gate[0:1, :] * mixed[...]).astype(jnp.bfloat16)


def fused(n, latent, t_index, mod_table, w_qkv, w_out):
    mod_table = jnp.transpose(mod_table, (1, 0, 2))
    rows, feats = latent.shape
    depth, cols = w_qkv.shape
    depth_o, cols_o = w_out.shape
    heads = cols // (3 * HEAD_DIM)
    bf, f32 = jnp.bfloat16, jnp.float32
    dma = pltpu.SemaphoreType.DMA
    return pl.pallas_call(
        functools.partial(fused_kernel, n),
        out_shape=pltpu.VMEM((rows, feats), bf),
        in_specs=[
            pl.BlockSpec(memory_space=pltpu.HBM),
            pl.BlockSpec(memory_space=pltpu.SMEM),
            pl.BlockSpec(memory_space=pltpu.HBM),
            pl.BlockSpec(memory_space=pltpu.HBM),
            pl.BlockSpec(memory_space=pltpu.HBM),
        ],
        out_specs=pl.BlockSpec(memory_space=pltpu.VMEM),
        scratch_shapes=[
            pltpu.VMEM((n * rows, feats), bf),
            pltpu.VMEM(mod_table.shape, bf),
            pltpu.VMEM((n, 16, feats), bf),
            pltpu.VMEM((n, 8, rows), f32),
            pltpu.VMEM((8, feats), f32),
            pltpu.VMEM((n, 2 * depth // n, cols), bf),
            pltpu.VMEM((n, 2 * depth_o // n, cols_o), bf),
            pltpu.VMEM((rows, cols), f32),
            pltpu.VMEM((2, rows, LANES), f32),
            pltpu.VMEM((rows, cols), bf),
            pltpu.VMEM((heads, rows, 2 * HEAD_DIM), bf),
            pltpu.VMEM((n * heads * rows, HEAD_DIM), bf),
            pltpu.VMEM((rows, cols_o), f32),
            dma((PIECES[0],)),
            dma,
            dma((2, 3)),
            dma((n * sum(PIECES),)),
            dma,
            dma,
            dma,
            dma,
            dma,
            dma,
            dma,
            dma,
            dma,
            dma((heads,)),
            pltpu.SemaphoreType.REGULAR((3,)),
        ],
        compiler_params=pltpu.CompilerParams(
            collective_id=0, has_side_effects=True, vmem_limit_bytes=24 * 1024 * 1024
        ),
    )(*(pltpu.with_memory_space_constraint(v, pltpu.HBM) if v.ndim > 1 else v for v in (latent, t_index, mod_table, w_qkv, w_out)))


def solution(mesh):
    in_specs = (
        P(("groups", "seq", "section"), "mp"),
        P("groups"),
        P(None, None, "mp"),
        P("section", "mp"),
        P("section", "mp"),
    )
    out_specs = P(("groups", "seq", "section"), "mp")
    n = mesh.shape["mp"]

    def body(latent, t_index, mod_table, w_qkv, w_out):
        heads = w_qkv.shape[1] // (3 * HEAD_DIM)
        fits = (
            mesh.shape["seq"] == 1
            and mesh.shape["section"] == 2
            and n % WIDE == 0
            and n == 4 * WIDE
            and heads == 2
            and latent.shape[0] <= latent.shape[1]
            and latent.shape[0] % 256 == 0
        )
        if not fits:
            return local(latent, t_index, mod_table, w_qkv, w_out)
        return fused(n, latent, t_index, mod_table, w_qkv, w_out)

    return jax.shard_map(body, mesh=mesh, in_specs=in_specs, out_specs=out_specs, check_vma=False)
```

```python
import functools
import math

import jax
import jax.numpy as jnp
from jax import lax
from jax.experimental import pallas as pl
from jax.experimental.pallas import tpu as pltpu
from jax.sharding import PartitionSpec as P

HEAD_DIM = 128
LANES = 128
WIDE = 2
PIECES = (4, 8)
MESH = pl.DeviceIdType.MESH


def layer_normed(values):
    mean_row = jnp.mean(values, axis=-1, keepdims=True)
    centred = values - mean_row
    variance = jnp.mean(centred * centred, axis=-1, keepdims=True)
    return centred * lax.rsqrt(variance + 1e-06)


def local(latent, t_index, mod_table, w_qkv, w_out):
    mod_local = lax.dynamic_index_in_dim(mod_table, t_index[0], 0, keepdims=False)
    features, mod_whole = (
        lax.all_gather(latent, "mp", axis=1, tiled=True),
        lax.all_gather(mod_local, "mp", axis=1, tiled=True),
    )
    mod_float = mod_whole.astype(jnp.float32)
    modulated = (
        layer_normed(features.astype(jnp.float32)) * (1.0 + mod_float[1]) + mod_float[0]
    ).astype(jnp.bfloat16)
    tok_rows = latent.shape[0]
    heads_dev = w_qkv.shape[1] // (3 * HEAD_DIM)
    qkv_full, out_full = (
        lax.all_gather(w_qkv, "section", axis=0, tiled=True),
        lax.all_gather(w_out, "section", axis=0, tiled=True),
    )
    projected = jnp.dot(modulated, qkv_full, preferred_element_type=jnp.float32).astype(
        jnp.bfloat16
    )
    grouped = projected.reshape(tok_rows, heads_dev, 3, HEAD_DIM)
    queries = grouped[:, :, 0]
    key_rows = grouped[:, :, 1]
    value_rows = grouped[:, :, 2]
    scale_factor = 1.0 / math.sqrt(HEAD_DIM)
    initial = (
        jnp.full((tok_rows, heads_dev), -1e30, jnp.float32),
        jnp.zeros((tok_rows, heads_dev), jnp.float32),
        jnp.zeros((tok_rows, heads_dev, HEAD_DIM), jnp.float32),
    )
    key_piece = lax.all_gather(key_rows, ("seq", "section"), axis=0, tiled=True)
    value_piece = lax.all_gather(value_rows, ("seq", "section"), axis=0, tiled=True)
    total_rows = key_piece.shape[0]
    block_rows = math.gcd(total_rows, 1024)

    def one_block(block_index, carried_block):
        running, totals, weighted = carried_block
        key_block = lax.dynamic_slice_in_dim(key_piece, block_index * block_rows, block_rows, 0)
        value_block = lax.dynamic_slice_in_dim(value_piece, block_index * block_rows, block_rows, 0)
        scores = (
            jnp.einsum("thd,khd->thk", queries, key_block, preferred_element_type=jnp.float32)
            * scale_factor
        )
        newest = jnp.maximum(running, jnp.max(scores, axis=-1))
        factor = jnp.exp(running - newest)
        weights = jnp.exp(scores - newest[..., None])
        totals = totals * factor + jnp.sum(weights, axis=-1)
        weighted = weighted * factor[..., None] + jnp.einsum(
            "thk,khd->thd",
            weights.astype(jnp.bfloat16),
            value_block,
            preferred_element_type=jnp.float32,
        )
        return (newest, totals, weighted)

    finished = lax.fori_loop(0, total_rows // block_rows, one_block, initial)
    attended = (
        (finished[2] / finished[1][..., None])
        .astype(jnp.bfloat16)
        .reshape(tok_rows, heads_dev * HEAD_DIM)
    )
    mixed_rows = jnp.dot(
        lax.all_gather(attended, "mp", axis=1, tiled=True),
        out_full,
        preferred_element_type=jnp.float32,
    )
    return (latent.astype(jnp.float32) + mod_local[2].astype(jnp.float32) * mixed_rows).astype(
        jnp.bfloat16
    )


def item_codes(deep):
    def pack(d, other, far):
        return (d * 2 + other) * 2 + far

    me, beside, idle = pack(0, 0, 0), pack(0, 1, 0), pack(deep, 0, 0)
    own = [pack(d, 0, 0) for d in range(deep)]
    cross = [pack(d, 1, 0) for d in range(deep)]
    far = [pack(d, 1, 1) for d in range(deep)]
    features = (
        [me, own[1], beside, own[2], cross[1]],
        [own[3], cross[2], cross[3], far[1], far[2], far[3]],
    )
    heads = (
        ([idle], [me]),
        ([me, own[1], beside, own[2], cross[1]], [own[1], beside, own[2], cross[1], cross[2]]),
        ([cross[2], own[3], pack(3, 0, 1), far[3]], [far[1], far[2], idle, idle]),
        ([cross[3]], [idle]),
    )
    return features, heads


def fused_kernel(
    n,
    x_hbm,
    t_ref,
    mod_hbm,
    wq_hbm,
    wo_hbm,
    out_ref,
    xs,
    table,
    mods,
    sums,
    gate,
    wq,
    wo,
    acc,
    stat,
    proj,
    pkv,
    att,
    mixed,
    own_sem,
    table_sem,
    ssem,
    rsem,
    mods_send,
    mods_recv,
    sums_send,
    sums_recv,
    wq_sem,
    wq_send,
    wo_sem,
    wo_send,
    kv_send,
    kv_recv,
    wave,
):
    me = lax.axis_index("mp")
    sec = lax.axis_index("section")
    other = 1 - sec
    deep = n // WIDE
    z, x = me // WIDE, me % WIDE
    rows, feats = x_hbm.shape
    piece_q = wq.shape[1]
    per_sec = n // 2
    piece_o = wo.shape[1]
    heads = wo.shape[1] // HEAD_DIM
    half = rows // 2
    above = z + 1 < deep
    below = z > 0
    at_end = jnp.logical_or(z == 0, z == deep - 1)
    beside = z * WIDE + (1 - x)
    UP, DOWN, CROSS = 0, 1, 2
    targets = (me + WIDE, me - WIDE, beside)
    into = jnp.where(2 * z < deep, 1, -1)
    inward = jnp.where(2 * z < deep, UP, DOWN)
    outer = jnp.where(2 * z < deep, DOWN, UP)
    next_in, second_in, next_out = (me + step * into * WIDE for step in (1, 2, -1))

    barrier = pltpu.get_barrier_semaphore()
    pl.semaphore_signal(barrier, inc=1, device_id={"mp": beside}, device_id_type=MESH)
    pl.semaphore_signal(barrier, inc=1, device_id={"section": other}, device_id_type=MESH)

    @pl.when(above)
    def _():
        pl.semaphore_signal(barrier, inc=1, device_id={"mp": me + WIDE}, device_id_type=MESH)

    @pl.when(below)
    def _():
        pl.semaphore_signal(barrier, inc=1, device_id={"mp": me - WIDE}, device_id_type=MESH)

    def own_copy(q):
        part = rows // PIECES[0]
        return pltpu.make_async_copy(
            x_hbm.at[pl.ds(q * part, part)],
            xs.at[pl.ds(pl.multiple_of(me * rows + q * part, part), part)],
            own_sem.at[q],
        )

    for q in range(PIECES[0]):
        own_copy(q).start()
    table_copy = pltpu.make_async_copy(mod_hbm, table, table_sem)
    table_copy.start()

    def wq_local(i):
        p = sec * per_sec + i
        return pltpu.make_async_copy(
            wq_hbm.at[pl.ds(i * piece_q, piece_q)], wq.at[p], wq_sem
        )

    def wo_local(i):
        return pltpu.make_async_copy(
            wo_hbm.at[pl.ds(i * piece_o, piece_o)],
            wo.at[sec * per_sec + i],
            wo_sem,
        )

    def wq_remote(i):
        p = sec * per_sec + i
        return pltpu.make_async_remote_copy(
            src_ref=wq_hbm.at[pl.ds(i * piece_q, piece_q)],
            dst_ref=wq.at[p],
            send_sem=wq_send,
            recv_sem=wq_sem,
            device_id={"section": other},
            device_id_type=MESH,
        )

    def wo_remote(i):
        p = sec * per_sec + i
        return pltpu.make_async_remote_copy(
            src_ref=wo_hbm.at[pl.ds(i * piece_o, piece_o)],
            dst_ref=wo.at[p],
            send_sem=wo_send,
            recv_sem=wo_sem,
            device_id={"section": other},
            device_id_type=MESH,
        )

    parts = tuple(rows * (1, heads)[phase] // PIECES[phase] for phase in range(2))
    near_of = tuple(count // 2 for count in PIECES)
    subs = PIECES[1] // (2 * heads)

    def chunk(phase, src, q):
        part = parts[phase]
        if phase == 0:
            return xs.at[pl.ds(pl.multiple_of(src * rows + q * part, part), part), :]
        block = q // subs
        first = (src * heads + lax.rem(block, heads)) * rows
        first += (block // heads * subs + lax.rem(q, subs)) * part
        return att.at[pl.ds(pl.multiple_of(first, part), part), :]

    def arrival(phase, src, q, column):
        count, near = PIECES[phase], near_of[phase]
        row = src // WIDE
        along = row * count + q
        crossed = deep * count + row * (near + 1) + jnp.minimum(q, near)
        base = phase * deep * (PIECES[0] + near_of[0] + 1)
        return rsem.at[base + jnp.where(src % WIDE == column, along, crossed)]

    def hop(phase, src, q, direction, target=None):
        column = 1 - x if target is None and direction == CROSS else x
        return pltpu.make_async_remote_copy(
            src_ref=chunk(phase, src, q),
            dst_ref=chunk(phase, src, q),
            send_sem=ssem.at[phase, direction],
            recv_sem=arrival(phase, src, q, column),
            device_id={"mp": targets[direction] if target is None else target},
            device_id_type=MESH,
        )

    def landed(phase, src, q):
        piece = chunk(phase, src, q)
        return pltpu.make_async_copy(piece, piece, arrival(phase, src, q, x))

    def own_along(phase, slot):
        q = lax.rem(slot + jnp.where(at_end, near_of[phase], 0), PIECES[phase])

        @pl.when(above)
        def _():
            hop(phase, me, q, UP).start()

        @pl.when(below)
        def _():
            hop(phase, me, q, DOWN).start()

    pl.semaphore_wait(barrier, 2 + above.astype(jnp.int32) + below.astype(jnp.int32))

    def tell(which, target):
        pl.semaphore_signal(
            wave.at[which], inc=1, device_id={"mp": target}, device_id_type=MESH
        )

    def rise():
        @pl.when(z > 1)
        def _():
            pl.semaphore_wait(wave.at[UP], 1)

        @pl.when(jnp.logical_and(below, above))
        def _():
            tell(UP, me + WIDE)

    def sink():
        @pl.when(z < deep - 2)
        def _():
            pl.semaphore_wait(wave.at[DOWN], 1)

        @pl.when(jnp.logical_and(below, above))
        def _():
            tell(DOWN, me - WIDE)

    for slot in range(PIECES[0] - 1):
        if slot < near_of[0]:
            own_copy(slot).wait()
            own_copy(slot + near_of[0]).wait()
        hop(0, me, slot, CROSS).start()
        own_along(0, slot)

    for i in range(per_sec):
        wq_local(i).start()

    @pl.when(2 * z < deep)
    def _():
        rise()

    @pl.when(2 * z >= deep)
    def _():
        sink()

    mine = xs[pl.ds(me * rows, rows), :].astype(jnp.float32)
    table_copy.wait()

    def mod_row(j):
        entries = table[j].astype(jnp.float32)
        steps = lax.broadcasted_iota(jnp.int32, entries.shape, 0)
        chosen = jnp.where(steps == t_ref[0], entries, 0.0)
        return jnp.sum(chosen, axis=0, keepdims=True)

    mean_col = jnp.sum(mine, axis=1, keepdims=True) * (1.0 / feats)
    off = mine - mean_col
    m2_col = jnp.sum(off * off, axis=1, keepdims=True)
    mean_row = jnp.broadcast_to(mean_col, (rows, LANES)).T[0:1, :]
    m2_row = jnp.broadcast_to(m2_col, (rows, LANES)).T[0:1, :]
    mods[me, 0:2, :] = jnp.concatenate([mod_row(0), mod_row(1)], axis=0).astype(jnp.bfloat16)
    sums[me, 0:1, :] = mean_row
    sums[me, 1:2, :] = m2_row
    gate[0:1, :] = mod_row(2)

    @pl.when(2 * z < deep)
    def _():
        sink()

    @pl.when(2 * z >= deep)
    def _():
        rise()

    tell(CROSS, beside)
    pl.semaphore_wait(wave.at[CROSS], 1)

    def small_copies(step):
        return [
            pltpu.make_async_remote_copy(
                src_ref=held.at[me, pl.ds(0, 2)],
                dst_ref=held.at[me, pl.ds(0, 2)],
                send_sem=send_sem,
                recv_sem=recv_sem,
                device_id={"mp": lax.rem(me + step, n)},
                device_id_type=MESH,
            )
            for held, send_sem, recv_sem in (
                (sums, sums_send, sums_recv),
                (mods, mods_send, mods_recv),
            )
        ]

    def settled(ref, sem):
        pltpu.make_async_copy(ref, ref, sem).wait()

    for step in range(1, n):
        for copy in small_copies(step):
            copy.start()
    hop(0, me, PIECES[0] - 1, CROSS).start()
    own_along(0, PIECES[0] - 1)
    for i in range(per_sec):
        wq_remote(i).start()
    for i in range(per_sec):
        wo_local(i).start()
        wo_remote(i).start()
    acc[...] = jnp.zeros_like(acc)
    mixed[...] = jnp.zeros_like(mixed)

    feature_items, head_items = item_codes(deep)

    def lookup(table_of, j):
        found = table_of[0]
        for i in range(1, len(table_of)):
            found = jnp.where(j == i, table_of[i], found)
        return found

    def inside(sz):
        return jnp.logical_and(sz >= 0, sz < deep)

    def is_end(sz):
        return jnp.logical_or(sz == 0, sz == deep - 1)

    def item(phase, code, use_all, use_half):
        count, near = PIECES[phase], near_of[phase]
        far = lax.rem(code, 2) == 1
        crossed = lax.rem(code // 2, 2) == 1
        d = code // 4

        def one(i, carry):
            sz = z + (1 - 2 * i) * into * d
            end = is_end(sz)
            src = sz * WIDE + jnp.where(crossed, 1 - x, x)
            valid = jnp.logical_and(inside(sz), jnp.logical_or(jnp.logical_not(far), end))
            valid = jnp.logical_and(valid, jnp.logical_or(d > 0, i == 0))
            direct = jnp.logical_and(valid, jnp.logical_and(crossed, jnp.logical_not(far)))

            @pl.when(direct)
            def _():
                block = (xs, att)[phase].at[pl.ds(0, near * parts[phase])]
                settled(block, arrival(phase, src, near, x))

            whole = jnp.logical_and(direct, jnp.logical_not(end))
            if phase == 1:
                whole = jnp.logical_and(whole, d > 0)

            @pl.when(whole)
            def _():
                for q in range(near):
                    landed(phase, src, q).wait()

            unseen = d == deep - 1
            if phase == 1:
                unseen = d != deep - 2

            @pl.when(jnp.logical_and(jnp.logical_and(valid, far), unseen))
            def _():
                for q in range(near):
                    landed(phase, src, q).wait()

            halved = crossed
            if phase == 1:
                halved = jnp.logical_or(crossed, d == deep - 1)
            split = jnp.logical_and(halved, jnp.logical_and(end, d > 0))

            @pl.when(jnp.logical_and(valid, jnp.logical_not(split)))
            def _():
                use_all(src)

            @pl.when(jnp.logical_and(valid, split))
            def _():
                use_half(src, pl.multiple_of(jnp.where(far, 0, half), half))

            return carry

        lax.fori_loop(0, jnp.where(at_end, 1, 2), one, 0)

    def passing(t):
        count, near = PIECES[0], near_of[0]
        s, slot = 1 + t // count, lax.rem(t, count)
        for sign, onward, has in ((1, DOWN, below), (-1, UP, above)):
            sz = z + sign * s
            src = sz * WIDE + x
            end = is_end(sz)
            q = lax.rem(slot + jnp.where(end, near, 0), count)

            @pl.when(inside(sz))
            def _():
                landed(0, src, q).wait()

                @pl.when(has)
                def _():
                    hop(0, src, q, onward).start()

                @pl.when(jnp.logical_not(jnp.logical_and(q < near, end)))
                def _():
                    hop(0, src, q, CROSS).start()

        first = t - 1

        @pl.when(jnp.logical_and(at_end, jnp.logical_and(first >= 0, first < near)))
        def _():
            landed(0, beside, first).wait()
            hop(0, beside, first, inward, me + into * WIDE).start()

        for sign, onward in ((1, DOWN), (-1, UP)):
            d = deep - 1 - z if sign > 0 else z
            src = (z + sign * d) * WIDE + (1 - x)
            q = t - (count * d + 2 - d)
            passed = jnp.logical_and(d > 0, d < deep - 1)

            @pl.when(jnp.logical_and(passed, jnp.logical_and(q >= 0, q < near)))
            def _():
                landed(0, src, q).wait()
                hop(0, src, q, onward).start()

    def pass_on(sz, column, turns, to=(), across=()):
        src = sz * WIDE + column
        for q in turns:
            landed(1, src, q).wait()
            for direction, target in to:
                hop(1, src, q, direction, target).start()
            if q in across:
                hop(1, src, q, CROSS).start()

    every = list(range(PIECES[1]))
    far_half, near_half = every[: near_of[1]], every[near_of[1] :]
    to_next, to_second, to_outer = (inward, next_in), (inward, second_in), (outer, next_out)

    def relay_first():
        @pl.when(at_end)
        def _():
            pass_on(z + into, x, near_half, across=near_half)
            for one in far_half:
                pass_on(z, 1 - x, [one], to=[to_second])
                pass_on(z + into, x, [one])
            for q in near_half:
                hop(1, me, q, *to_next).start()
            for q in far_half:
                hop(1, beside, q, *to_next).start()
            pass_on(z + 2 * into, x, every, across=every)

        @pl.when(jnp.logical_not(at_end))
        def _():
            pass_on(z + into, x, every, to=[to_outer], across=every)
            pass_on(z, 1 - x, far_half, to=[to_outer])
            pass_on(z - into, x, far_half, to=[to_next])
            pass_on(z + 2 * into, x, near_half, to=[to_outer], across=near_half)
            for one in far_half:
                pass_on(z + 2 * into, x, [one], to=[to_outer])
                pass_on(z + 2 * into, 1 - x, [one], to=[to_outer])
            pass_on(z - into, x, near_half, across=near_half)

    def relay_last():
        @pl.when(at_end)
        def _():
            pass_on(z + 3 * into, x, near_half, across=near_half)

    def drain(phase):
        pieces, near = PIECES[phase], near_of[phase]

        def sent(direction, count):
            settled((xs, att)[phase].at[pl.ds(0, count * parts[phase])], ssem.at[phase, direction])

        for at in range(deep):

            @pl.when(z == at)
            def _():
                ends = at in (0, deep - 1)
                if phase == 0:
                    sent(CROSS, pieces * (deep - 1) + (near if ends else 0))
                else:
                    sent(CROSS, pieces * (deep - 1))
                if phase == 0:
                    up, down = pieces * (at + 1) + near, pieces * (deep - at) + near
                elif ends:
                    up = down = pieces + near + 2 * near
                else:
                    along = (pieces + near, 3 * pieces + 2 * near)
                    up, down = along if 2 * at < deep else along[::-1]
                if at < deep - 1:
                    sent(UP, up)
                if at > 0:
                    sent(DOWN, down)

    def run(phase, items, use_all, use_half):
        end_items, middle_items = items

        def one(i, carry):
            code = jnp.where(at_end, lookup(end_items, i), lookup(middle_items, i))
            item(phase, code, use_all, use_half)
            return carry

        lax.fori_loop(0, len(end_items), one, 0)

    def gather_features(use_all, use_half):
        steps, wait_steps = (deep - 1) * PIECES[0], PIECES[0] + PIECES[0] - 1
        items, tail = feature_items

        def quiet(t, carry):
            passing(t)
            return carry

        def busy(t, carry):
            item(0, lookup(items, t - wait_steps), use_all, use_half)
            passing(t)
            return carry

        until = wait_steps + len(items)
        lax.fori_loop(0, wait_steps, quiet, 0)
        statistics()
        lax.fori_loop(wait_steps, until, busy, 0)
        lax.fori_loop(until, steps, quiet, 0)
        run(0, (tail, tail), use_all, use_half)

    def gather_heads(use_all, use_half):
        run(1, head_items[0], use_all, use_half)
        relay_first()
        run(1, head_items[1], use_all, use_half)
        relay_last()
        run(1, head_items[2], use_all, use_half)
        drain(1)
        run(1, head_items[3], use_all, use_half)

    def statistics():
        settled(wq, wq_sem)
        settled(sums.at[pl.ds(0, n - 1), pl.ds(0, 2)], sums_recv)
        settled(mods.at[pl.ds(0, n - 1), pl.ds(0, 2)], mods_recv)
        total = jnp.zeros((1, rows), jnp.float32)
        for p in range(n):
            total = total + sums[p, 0:1, :]
        grand = total * (1.0 / n)
        m2 = jnp.zeros((1, rows), jnp.float32)
        for p in range(n):
            gap = sums[p, 0:1, :] - grand
            m2 = m2 + sums[p, 1:2, :] + feats * (gap * gap)
        inv = lax.rsqrt(m2 * (1.0 / (n * feats)) + 1e-06)
        stat[0] = jnp.broadcast_to(grand, (LANES, rows)).T
        stat[1] = jnp.broadcast_to(inv, (LANES, rows)).T

    def project(src, start, size):
        taken = pl.ds(start, size)
        mean, rstd = stat[0, taken, :], stat[1, taken, :]
        shift = mods[src, 0:1, :].astype(jnp.float32)
        scale = 1.0 + mods[src, 1:2, :].astype(jnp.float32)
        pieces = []
        for c in range(feats // LANES):
            cols = slice(c * LANES, (c + 1) * LANES)
            values = xs[pl.ds(src * rows + start, size), cols].astype(jnp.float32)
            pieces.append(
                ((values - mean) * rstd * scale[:, cols] + shift[:, cols]).astype(jnp.bfloat16)
            )
        acc[taken, :] += jnp.dot(
            jnp.concatenate(pieces, axis=1), wq[src], preferred_element_type=jnp.float32
        )

    gather_features(
        lambda src: project(src, 0, rows), lambda src, start: project(src, start, half)
    )

    def kv_copy(h):
        return pltpu.make_async_remote_copy(
            src_ref=proj.at[:, pl.ds((3 * h + 1) * HEAD_DIM, 2 * HEAD_DIM)],
            dst_ref=pkv.at[h],
            send_sem=kv_send,
            recv_sem=kv_recv.at[h],
            device_id={"section": other},
            device_id_type=MESH,
        )

    for h in range(heads):
        cols = slice((3 * h + 1) * HEAD_DIM, (3 * h + 3) * HEAD_DIM)
        proj[:, cols] = acc[:, cols].astype(jnp.bfloat16)
        kv_copy(h).start()

    factor = math.log2(math.e) / math.sqrt(HEAD_DIM)
    contract = (((1,), (1,)), ((), ()))
    def attend(taken):
        raw, tops, sides = [], [], []
        for h in range(heads):
            base = 3 * h * HEAD_DIM
            queries = acc[taken, base : base + HEAD_DIM].astype(jnp.bfloat16)
            own_k = proj[:, base + HEAD_DIM : base + 2 * HEAD_DIM]
            far_k = pkv[h, :, 0:HEAD_DIM]
            raw.append(
                [
                    lax.dot_general(queries, keys, contract, preferred_element_type=jnp.float32)
                    for keys in (own_k, far_k)
                ]
            )
        for own_s, far_s in raw:
            tops.append(
                jnp.maximum(
                    jnp.max(own_s, axis=1, keepdims=True), jnp.max(far_s, axis=1, keepdims=True)
                )
            )
        for pair, top in zip(raw, tops):
            sides.append([jnp.exp2((scores - top) * factor) for scores in pair])
        results = []
        for h, (e_own, e_far) in enumerate(sides):
            base = 3 * h * HEAD_DIM
            own_v = proj[:, base + 2 * HEAD_DIM : base + 3 * HEAD_DIM]
            far_v = pkv[h, :, HEAD_DIM : 2 * HEAD_DIM]
            norm = jnp.sum(e_own, axis=1, keepdims=True) + jnp.sum(e_far, axis=1, keepdims=True)
            weighted = jnp.dot(
                e_own.astype(jnp.bfloat16), own_v, preferred_element_type=jnp.float32
            ) + jnp.dot(e_far.astype(jnp.bfloat16), far_v, preferred_element_type=jnp.float32)
            results.append((weighted / norm).astype(jnp.bfloat16))
        return results

    for h in range(heads):
        kv_copy(h).wait_recv()
    for turn, first_half in ((far_half, True), (near_half, False)):
        start = 0 if first_half else half
        for h, result in enumerate(attend(pl.ds(start, half))):
            att[pl.ds(pl.multiple_of((me * heads + h) * rows + start, half), half), :] = result
        for q in turn:
            hop(1, me, q, CROSS).start()

        @pl.when(jnp.logical_not(at_end))
        def _():
            for q in turn:
                hop(1, me, q, *to_next).start()
                hop(1, me, q, *to_outer).start()

        @pl.when(at_end)
        def _():
            for q in turn:
                hop(1, me, q, *(to_next if first_half else to_second)).start()

    def settle():
        settled(wo, wo_sem)
        settled(sums.at[pl.ds(0, n - 1), pl.ds(0, 2)], sums_send)
        settled(mods.at[pl.ds(0, n - 1), pl.ds(0, 2)], mods_send)
        settled(wq.at[pl.ds(0, per_sec)], wq_send)
        settled(wo.at[pl.ds(0, per_sec)], wo_send)
        settled(pkv, kv_send)
        drain(0)

    def mix(src, start, size):
        taken = pl.ds(start, size)
        joined = jnp.concatenate(
            [att[pl.ds((src * heads + h) * rows + start, size), :] for h in range(heads)], axis=1
        )
        mixed[taken, :] += jnp.dot(joined, wo[src], preferred_element_type=jnp.float32)

    settle()
    gather_heads(lambda src: mix(src, 0, rows), lambda src, start: mix(src, start, half))

    out_ref[...] = (xs[pl.ds(me * rows, rows), :].astype(jnp.float32) + gate[0:1, :] * mixed[...]).astype(jnp.bfloat16)


def fused(n, latent, t_index, mod_table, w_qkv, w_out):
    mod_table = jnp.transpose(mod_table, (1, 0, 2))
    rows, feats = latent.shape
    depth, cols = w_qkv.shape
    depth_o, cols_o = w_out.shape
    heads = cols // (3 * HEAD_DIM)
    bf, f32 = jnp.bfloat16, jnp.float32
    dma = pltpu.SemaphoreType.DMA
    return pl.pallas_call(
        functools.partial(fused_kernel, n),
        out_shape=pltpu.VMEM((rows, feats), bf),
        in_specs=[
            pl.BlockSpec(memory_space=pltpu.HBM),
            pl.BlockSpec(memory_space=pltpu.SMEM),
            pl.BlockSpec(memory_space=pltpu.HBM),
            pl.BlockSpec(memory_space=pltpu.HBM),
            pl.BlockSpec(memory_space=pltpu.HBM),
        ],
        out_specs=pl.BlockSpec(memory_space=pltpu.VMEM),
        scratch_shapes=[
            pltpu.VMEM((n * rows, feats), bf),
            pltpu.VMEM(mod_table.shape, bf),
            pltpu.VMEM((n, 16, feats), bf),
            pltpu.VMEM((n, 8, rows), f32),
            pltpu.VMEM((8, feats), f32),
            pltpu.VMEM((n, 2 * depth // n, cols), bf),
            pltpu.VMEM((n, 2 * depth_o // n, cols_o), bf),
            pltpu.VMEM((rows, cols), f32),
            pltpu.VMEM((2, rows, LANES), f32),
            pltpu.VMEM((rows, cols), bf),
            pltpu.VMEM((heads, rows, 2 * HEAD_DIM), bf),
            pltpu.VMEM((n * heads * rows, HEAD_DIM), bf),
            pltpu.VMEM((rows, cols_o), f32),
            dma((PIECES[0],)),
            dma,
            dma((2, 3)),
            dma((n // WIDE * sum(count + count // 2 + 1 for count in PIECES),)),
            dma,
            dma,
            dma,
            dma,
            dma,
            dma,
            dma,
            dma,
            dma,
            dma((heads,)),
            pltpu.SemaphoreType.REGULAR((3,)),
        ],
        compiler_params=pltpu.CompilerParams(
            collective_id=0, has_side_effects=True, vmem_limit_bytes=24 * 1024 * 1024
        ),
    )(*(pltpu.with_memory_space_constraint(v, pltpu.HBM) if v.ndim > 1 else v for v in (latent, t_index, mod_table, w_qkv, w_out)))


def solution(mesh):
    in_specs = (
        P(("groups", "seq", "section"), "mp"),
        P("groups"),
        P(None, None, "mp"),
        P("section", "mp"),
        P("section", "mp"),
    )
    out_specs = P(("groups", "seq", "section"), "mp")
    n = mesh.shape["mp"]

    def body(latent, t_index, mod_table, w_qkv, w_out):
        heads = w_qkv.shape[1] // (3 * HEAD_DIM)
        fits = (
            mesh.shape["seq"] == 1
            and mesh.shape["section"] == 2
            and n % WIDE == 0
            and n == 4 * WIDE
            and heads == 2
            and latent.shape[0] <= latent.shape[1]
            and latent.shape[0] % 256 == 0
        )
        if not fits:
            return local(latent, t_index, mod_table, w_qkv, w_out)
        return fused(n, latent, t_index, mod_table, w_qkv, w_out)

    return jax.shard_map(body, mesh=mesh, in_specs=in_specs, out_specs=out_specs, check_vma=False)
```
